32 devices in a mesh: cx: 4 (over z), cy: 8 (over y, x, core).
Axes of the slice: x: 2, y: 2, z: 4, core: 2. Of those that a mesh axis runs over, the one named last changes fastest.
Arguments:
- latent: float32 [64, 128, 256], P('cx', 'cy'), may hold values from -6 to 6
- observed: float32 [32768], P(('cx', 'cy')), may hold values from -12 to 12
- sigma: float32 [32768], P(('cx', 'cy')), may hold values from 0.5 to 1.5
- response: bfloat16 [16384, 64, 128], P(('cx', 'cy')), may hold values from -0.375 to 0.375
- offsets: int32 [64, 16384], P(None, ('cx', 'cy')), may hold values from 0 to 254
- fractions: float32 [64, 16384], P(None, ('cx', 'cy')), may hold values from 0 to 1
- tile_group: int32 [16384], P(('cx', 'cy')), may hold values from 0 to 7
- tile_slot: int32 [16384], P(('cx', 'cy')), may hold values from 0 to 511, as said below
- send_index: int32 [32, 32, 16], P(('cx', 'cy')), may hold values from -1 to 255, as said below
Outputs:
- gradient: float32 [64, 128, 256], P('cx', 'cy')
- predicted: float32 [32768], P(('cx', 'cy'))
The draws below stay inside these ranges and needn't reach their ends.
Inputs may be any that keep to these rules, and one draw needn't show every extreme that they name: `send_index`: entries are local column numbers of the sending device, or -1 for an empty slot; for each sender and receiver the used slots come first, 8 to 16 of them; every sender uses all 16 slots for some receiver, and some receiver gets all 16 slots from every sender. `tile_slot`: tile slot q names slot q % 16 from sender q // 16, a slot that this sender uses for this device.
All inputs are finite; a program needn't handle non-finite values.
Results may differ from the reference program's by a relative error of at most 0.0036.
Values may be sent and summed in bfloat16 or wider, within the bound.
No kernel may reach another device: no remote copies, remote signals or barrier semaphores. Data moves between devices by JAX's collectives and lax.ppermute only.
A program may use at most 64 MiB of HBM per device.

```python
import math
import jax
import jax.numpy as jnp
from jax import lax

CXV = 16
CYV = 16
NZ = 256
STAR_TILE = 128
SAMPLES = 64
NDEV = 32
TILES_DEV = 512
CAP = 16
G_DEV = 8
NX = 64
NY = 128
TILES = 16384
STARS = 32768
N_CX = 4
N_CY = 8


def pair_counts(key):
    counts = jax.random.randint(jax.random.fold_in(key, 101), (NDEV, NDEV), (CAP + 1) // 2, CAP + 1)
    chosen = jax.random.randint(jax.random.fold_in(key, 202), (NDEV,), 0, NDEV)
    full_owner = jax.random.randint(jax.random.fold_in(key, 303), (), 0, NDEV)
    owners = jnp.arange(NDEV)[None, :]
    filled = (chosen[:, None] == owners) | (owners == full_owner)
    return jnp.where(filled, CAP, counts)


def used_slots(key):
    counts = pair_counts(key)
    return jnp.arange(CAP)[None, None, :] < counts[:, :, None]


def draw_send_index(key, part):
    used_mask = used_slots(key)
    flat_used = used_mask.reshape(NDEV, NDEV * CAP).astype(jnp.int32)
    used_rank = jnp.cumsum(flat_used, axis=1) - 1
    row_keys = jax.random.split(jax.random.fold_in(key, 404), NDEV)
    shuffled = jax.vmap(lambda row_key: jax.random.permutation(row_key, CXV * CYV))(row_keys)
    column_picks = jnp.take_along_axis(shuffled, jnp.maximum(used_rank, 0) % (CXV * CYV), axis=1)
    result = jnp.where(flat_used > 0, column_picks, -1)
    return result.reshape(NDEV, NDEV, CAP).astype(jnp.int32)


def draw_tile_slot(key, part):
    used_mask = used_slots(key)
    by_owner = used_mask.transpose(1, 0, 2).reshape(NDEV, NDEV * CAP)
    slot_ids = jnp.arange(NDEV * CAP).astype(jnp.int32)
    scores = jnp.where(by_owner, 0, NDEV * CAP).astype(jnp.int32) + slot_ids[None, :]
    slot_order = jnp.argsort(scores, axis=1, stable=True).astype(jnp.int32)
    used_count = jnp.sum(by_owner.astype(jnp.int32), axis=1)
    row_keys = jax.random.split(jax.random.fold_in(key, 505), NDEV)
    shuffled = jax.vmap(lambda row_key: jax.random.permutation(row_key, TILES_DEV))(row_keys)
    chosen_rank = shuffled % used_count[:, None]
    tile_slots = jnp.take_along_axis(slot_order, chosen_rank, axis=1)
    return tile_slots.reshape(-1).astype(jnp.int32)


def set_ends(array, own_key, low, high):
    longest = array.shape.index(max(array.shape))
    spots = []
    for shift in (0, 1):
        where = [jax.random.randint(jax.random.fold_in(own_key, axis), (), 0, length) for axis, length in enumerate(array.shape)]
        where[longest] = (where[longest] + shift) % array.shape[longest]
        spots.append(tuple(where))
    return array.at[spots[0]].set(low).at[spots[1]].set(high)


def shard_levels(own_key, dims, shards, smallest, high):
    loudness, own = 1.0, jax.random.fold_in(own_key, 6)
    for axis_at, parts in shards:
        steps = jnp.exp(jax.random.uniform(jax.random.fold_in(own, axis_at), (parts,), jnp.float32, smallest / len(shards), high / len(shards)))
        loudness = loudness * jnp.repeat(steps, dims[axis_at] // parts).reshape([-1 if axis == axis_at else 1 for axis in range(len(dims))])
    return loudness


def bell_draw(own_key, shape, spread, bound, shards=(), kind=jnp.bfloat16):
    values = spread * jax.random.normal(own_key, shape, jnp.float32)
    if shards:
        values = values * shard_levels(own_key, shape, shards, -0.22, 0.18)
    return jnp.clip(values, -bound, bound).astype(kind)


def setup_inputs(seed: int = 0) -> dict:
    key_of = jax.random.split(jax.random.key(seed), 10)
    latent = bell_draw(key_of[0], (NX, NY, NZ), 1.0, 6.0, ((0, 4), (1, 8)), jnp.float32)
    observed = bell_draw(key_of[1], (STARS,), 2.0, 12.0, ((0, 32),), jnp.float32)
    sigma = jnp.clip(jnp.exp(math.log(1.5) - 1.0986123 * jax.random.uniform(key_of[2], (STARS,), jnp.float32) ** shard_levels(key_of[2], (STARS,), ((0, 32),), -0.2, 0.2)), 0.5, 1.5)
    response = bell_draw(key_of[3], (TILES, SAMPLES, STAR_TILE), (4 * SAMPLES) ** -0.5, 0.375, ((0, 32),))
    offsets = set_ends(jax.random.randint(key_of[4], (SAMPLES, TILES), 0, NZ - 1), jax.random.fold_in(key_of[4], 1), 0, (NZ - 1) - 1).astype(jnp.int32)
    fractions = jnp.clip(1.0 * jax.random.uniform(key_of[5], (SAMPLES, TILES), jnp.float32) ** shard_levels(key_of[5], (SAMPLES, TILES), ((1, 32),), -0.2, 0.2), 0.0, 1.0)
    tile_group = set_ends(jax.random.randint(key_of[6], (TILES,), 0, G_DEV), jax.random.fold_in(key_of[6], 1), 0, G_DEV - 1).astype(jnp.int32)
    tile_slot = draw_tile_slot(jax.random.fold_in(key_of[9], 71), 0)
    send_index = draw_send_index(jax.random.fold_in(key_of[9], 71), 0)
    return {"latent": latent, "observed": observed, "sigma": sigma, "response": response, "offsets": offsets, "fractions": fractions, "tile_group": tile_group, "tile_slot": tile_slot, "send_index": send_index}


def kernel_taps():
    shifts = jnp.arange(-16, 17).astype(jnp.float32)
    scaled = jnp.sqrt(jnp.float32(3.0)) * jnp.abs(shifts) / 8.0
    raw_taps = (1.0 + scaled) * jnp.exp(-scaled)
    return 0.8 * raw_taps / jnp.sqrt(jnp.sum(raw_taps * raw_taps))

def taps_along(values, along, kernel):
    length = values.shape[along]
    padding = [(0, 0), (0, 0), (0, 0)]
    padding[along] = (16, 16)
    widened = jnp.pad(values, padding)
    summed = jnp.zeros_like(values)
    for shift_at in range(33):
        summed = summed + kernel[shift_at] * lax.slice_in_dim(widened, shift_at, shift_at + length, axis=along)
    return summed

def smooth(values, kernel):
    return taps_along(taps_along(taps_along(values, 0, kernel), 1, kernel), 2, kernel)

def cone_work(inputs):
    received, resp, tile_offsets, tile_fracs, groups, slots, stars_obs, stars_sig = inputs
    sample_at = slots[:, None] * NZ + tile_offsets
    lower = received[sample_at].astype(jnp.float32)
    upper = received[sample_at + 1].astype(jnp.float32)
    samples = ((1.0 - tile_fracs) * lower + tile_fracs * upper).astype(jnp.bfloat16)
    tile_pred = jnp.einsum('tks,tk->ts', resp.astype(jnp.float32), samples.astype(jnp.float32))
    predicted = jax.ops.segment_sum(tile_pred, groups, num_segments=G_DEV)
    resid = (predicted - stars_obs) / (stars_sig * stars_sig)
    tile_resid = resid[groups].astype(jnp.bfloat16)
    back = jnp.einsum('tks,ts->tk', resp.astype(jnp.float32), tile_resid.astype(jnp.float32))
    flat_grad = jnp.zeros((NDEV * CAP * NZ,), jnp.float32)
    flat_grad = flat_grad.at[sample_at].add((1.0 - tile_fracs) * back)
    flat_grad = flat_grad.at[sample_at + 1].add(tile_fracs * back)
    return (predicted.reshape(-1), flat_grad)

def owner_sum(inputs):
    grads, targets = inputs
    summed = jax.ops.segment_sum(grads.reshape(-1, NZ), targets.reshape(-1), num_segments=CXV * CYV + 1)
    return summed[:CXV * CYV]

def reference(latent, observed, sigma, response, offsets, fractions, tile_group, tile_slot, send_index):
    kernel = kernel_taps()
    density = jnp.exp(smooth(latent, kernel))
    columns = density.reshape(N_CX, CXV, N_CY, CYV, NZ).transpose(0, 2, 1, 3, 4).reshape(NDEV, CXV * CYV, NZ)
    sent = columns.astype(jnp.bfloat16)
    valid = send_index >= 0
    safe_rows = jnp.maximum(send_index, 0)
    packed = jax.vmap(lambda owned, rows: owned[rows])(sent, safe_rows)
    packed = jnp.where(valid[..., None], packed, jnp.zeros((), jnp.bfloat16))
    blocks = packed.transpose(1, 0, 2, 3).reshape(NDEV, NDEV * CAP * NZ)
    inputs = (blocks, response.reshape(NDEV, TILES_DEV, SAMPLES, STAR_TILE), offsets.reshape(SAMPLES, NDEV, TILES_DEV).transpose(1, 2, 0).astype(jnp.int32), fractions.reshape(SAMPLES, NDEV, TILES_DEV).transpose(1, 2, 0), tile_group.reshape(NDEV, TILES_DEV).astype(jnp.int32), tile_slot.reshape(NDEV, TILES_DEV).astype(jnp.int32), observed.reshape(NDEV, G_DEV, STAR_TILE), sigma.reshape(NDEV, G_DEV, STAR_TILE))
    predicted, slot_grad = lax.map(cone_work, inputs)
    by_source = slot_grad.reshape(NDEV, NDEV, CAP, NZ).transpose(1, 0, 2, 3)
    targets = jnp.where(valid, safe_rows, CXV * CYV).astype(jnp.int32)
    column_grad = lax.map(owner_sum, (by_source, targets))
    dens_grad = column_grad.reshape(N_CX, N_CY, CXV, CYV, NZ).transpose(0, 2, 1, 3, 4).reshape(NX, NY, NZ)
    gradient = latent + smooth(density * dens_grad, kernel)
    return (gradient, predicted.reshape(-1))
```

```python
import functools
import math

import jax
import jax.numpy as jnp
from jax import lax
from jax.experimental import pallas as pl
from jax.experimental.pallas import tpu as pltpu
from jax.sharding import PartitionSpec as P

REACH = 16
LANES = 128
F32 = jnp.float32
BF16 = jnp.bfloat16
HALO = BF16


def tap_scale():
    total = 0.0
    for shift in range(-REACH, REACH + 1):
        a = math.sqrt(3.0) * abs(shift) / 8.0
        total += ((1.0 + a) * math.exp(-a)) ** 2
    return 0.8 / math.sqrt(total)


def split(values):
    high = values.astype(BF16)
    low = (values - high.astype(F32)).astype(BF16)
    return high, low


def mm(a, b):
    return jnp.dot(a, b, preferred_element_type=F32)


def mm_nt(a, b):
    return lax.dot_general(a, b, (((1,), (1,)), ((), ())), preferred_element_type=F32)


def iota(shape, dim):
    return lax.broadcasted_iota(jnp.int32, shape, dim)


def apply_left(mat_high, mat_low, values):
    if values.dtype == BF16:
        return mm(mat_high, values) + mm(mat_low, values)
    high, low = split(values)
    return mm(mat_high, high) + (mm(mat_high, low) + mm(mat_low, high))


def apply_right(values, mat_high, mat_low):
    high, low = split(values)
    return mm(high, mat_high) + (mm(low, mat_high) + mm(high, mat_low))


def call(body, outs, *args, scratch=(), limit=16, flops=0, name=None):
    shapes = [jax.ShapeDtypeStruct(s, d) for s, d in outs]
    moved = sum(math.prod(a.shape) * a.dtype.itemsize for a in args) + sum(
        math.prod(s.shape) * s.dtype.itemsize for s in shapes
    )
    return pl.pallas_call(
        body,
        out_shape=shapes,
        in_specs=[pl.BlockSpec(memory_space=pltpu.VMEM)] * len(args),
        out_specs=[pl.BlockSpec(memory_space=pltpu.VMEM)] * len(shapes),
        scratch_shapes=list(scratch),
        compiler_params=pltpu.CompilerParams(vmem_limit_bytes=limit << 20),
        cost_estimate=pl.CostEstimate(flops=flops, bytes_accessed=moved, transcendentals=0),
        name=name,
    )(*args)


def taps_matrix(distance, kept):
    a = (math.sqrt(3.0) / 8.0) * jnp.abs(distance).astype(F32)
    value = (tap_scale() * (1.0 + a)) * jnp.exp(-a)
    return jnp.where(kept & (jnp.abs(distance) <= REACH), value, 0.0)


def operators_body(rows_x, rows_y, depth, hx_ref, hy_ref, hz_ref):
    cells = rows_x * rows_y
    out = iota((cells, cells), 0)
    inp = iota((cells, cells), 1)
    out_x, out_y = out // rows_y, out % rows_y
    inp_x, inp_y = inp // rows_y, inp % rows_y
    for at, block in enumerate((0, 1, -1)):
        high, low = split(taps_matrix(out_x - inp_x + block * rows_x, out_y == inp_y))
        hx_ref[2 * at], hx_ref[2 * at + 1] = high, low
        high, low = split(taps_matrix(out_y - inp_y + block * rows_y, out_x == inp_x))
        hy_ref[2 * at], hy_ref[2 * at + 1] = high, low
    shift = iota((depth, depth), 0) - iota((depth, depth), 1)
    high, low = split(taps_matrix(shift, shift == shift))
    hz_ref[0], hz_ref[1] = high, low


def one_hot(hits):
    return jnp.where(hits, 1.0, 0.0).astype(BF16)


def tables_body(
    off_ref, frac_ref, group_ref, slot_ref, send_ref,
    idx_ref, w_ref, grp_ref, take_ref, give_ref, pack_ref, sum_ref, keep,
):
    tiles = off_ref.shape[1]
    slots = take_ref.shape[1]
    cells = pack_ref.shape[1]
    off = off_ref[...]
    frac = frac_ref[...]
    idx_ref[...] = jnp.concatenate([off, off + 1], axis=0).T
    w_ref[...] = jnp.concatenate([1.0 - frac, frac], axis=0).T
    keep[...] = jnp.broadcast_to(group_ref[...], (LANES, tiles)).T
    first = iota((tiles // 2, LANES), 1) < LANES // 2
    grp_ref[...] = jnp.where(
        first, keep[pl.ds(0, tiles // 2, 2), :], keep[pl.ds(1, tiles // 2, 2), :]
    )
    slot = slot_ref[...]
    wide = jnp.broadcast_to(slot, (LANES, tiles)).T
    for at in range(0, slots, LANES):
        take_ref[:, at : at + LANES] = one_hot(wide == iota((tiles, LANES), 1) + at)
    give_ref[...] = one_hot(jnp.broadcast_to(slot, (slots, tiles)) == iota((slots, tiles), 0))
    send = send_ref[...]
    wide = jnp.broadcast_to(send, (LANES, slots)).T
    for at in range(0, cells, LANES):
        pack_ref[:, at : at + LANES] = one_hot(wide == iota((slots, LANES), 1) + at)
    sum_ref[...] = one_hot(jnp.broadcast_to(send, (cells, slots)) == iota((cells, slots), 0))


def three(mats_ref, own, before, after):
    total = apply_left(mats_ref[0], mats_ref[1], own)
    total += apply_left(mats_ref[2], mats_ref[3], before)
    return total + apply_left(mats_ref[4], mats_ref[5], after)


def first_body(own_ref, before_ref, after_ref, mats_ref, out_ref, *sent_ref):
    out = three(mats_ref, own_ref[...], before_ref[...], after_ref[...])
    out_ref[...] = out
    for ref in sent_ref:
        ref[...] = out.astype(ref.dtype)


def density_body(own_ref, before_ref, after_ref, mats_ref, hz_ref, pack_ref, dens_ref, packed_ref):
    out = three(mats_ref, own_ref[...], before_ref[...], after_ref[...])
    dens = jnp.exp(apply_right(out, hz_ref[0], hz_ref[1]))
    dens_ref[...] = dens
    packed_ref[...] = mm(pack_ref[...], dens.astype(BF16)).astype(BF16)


def owner_body(sum_ref, back_ref, dens_ref, hz_ref, out_ref, sent_ref):
    grad = dens_ref[...] * mm(sum_ref[...], back_ref[...])
    out = apply_right(grad, hz_ref[0], hz_ref[1])
    out_ref[...] = out
    sent_ref[...] = out.astype(sent_ref.dtype)


def last_body(own_ref, before_ref, after_ref, mats_ref, latent_ref, out_ref):
    out_ref[...] = latent_ref[...] + three(mats_ref, own_ref[...], before_ref[...], after_ref[...])


def cone_body(
    got_ref, resp_ref, idx_ref, w_ref, grp_ref, take_ref, give_ref, obs_ref, sig_ref,
    pred_ref, grad_ref, both, pairs, weights, cells,
):
    tiles, samples, star_tile = resp_ref.shape
    depth = got_ref.shape[1]
    groups = obs_ref.shape[0]
    half = LANES // 2
    layers = depth // LANES
    step_pairs = 8
    step_tiles = 2 * step_pairs
    steps = tiles // step_tiles
    idx = idx_ref[...]
    columns = mm(take_ref[...], got_ref[...])
    value = jnp.zeros((tiles, LANES), F32)
    for at in range(layers):
        piece = jnp.take_along_axis(columns[:, at * LANES : (at + 1) * LANES], idx % LANES, axis=1)
        value = jnp.where(idx // LANES == at, piece, value)
    value = w_ref[...] * value
    both[...] = value + pltpu.roll(value, half, 1)
    first = iota((tiles // 2, LANES), 1) < half
    pairs[...] = jnp.where(
        first, both[pl.ds(0, tiles // 2, 2), :], both[pl.ds(1, tiles // 2, 2), :]
    )
    group_at = iota((groups, LANES), 0)

    def rows_of(ref, step):
        return ref[pl.ds(pl.multiple_of(step * step_tiles, step_tiles), step_tiles)].reshape(
            step_tiles * samples, star_tile
        )

    def pair_rows(ref, step):
        return ref[pl.ds(pl.multiple_of(step * step_pairs, step_pairs), step_pairs), :]

    def predict(step, total):
        pair = pair_rows(pairs, step)
        group = pair_rows(grp_ref, step)
        left = [
            jnp.where(group[i : i + 1] == group_at, pair[i : i + 1], 0.0)
            for i in range(step_pairs)
        ]
        return total + mm(jnp.concatenate(left, axis=1).astype(BF16), rows_of(resp_ref, step))

    pred = lax.fori_loop(0, steps, predict, jnp.zeros((groups, star_tile), F32))
    pred_ref[...] = pred
    sig = sig_ref[...]
    resid = ((pred - obs_ref[...]) / (sig * sig)).astype(BF16)
    rows = 2 * layers
    at_row = iota((2 * rows, LANES), 0)
    row_layer = at_row % layers
    row_tile = (at_row % rows) // layers
    row_high = at_row < rows
    lane_first = iota((step_pairs, LANES), 1) < half
    level = [(iota((16, LANES), 0) + 16 * k).astype(F32).astype(BF16) for k in range(LANES // 16)]
    one = jnp.ones((16, LANES), BF16)
    zero = jnp.zeros((16, LANES), BF16)

    def backward(step, carry):
        group = pair_rows(grp_ref, step)
        back = mm_nt(resid, rows_of(resp_ref, step))
        picked = [
            jnp.sum(
                jnp.where(group[i : i + 1] == group_at, back[:, i * LANES : (i + 1) * LANES], 0.0),
                axis=0, keepdims=True,
            )
            for i in range(step_pairs)
        ]
        picked = jnp.concatenate(picked, axis=0)
        swapped = pltpu.roll(picked, half, 1)
        base = pl.multiple_of(step * step_tiles, step_tiles)
        even = jnp.where(lane_first, picked, swapped) * w_ref[pl.ds(base, step_pairs, 2), :]
        odd = jnp.where(lane_first, swapped, picked) * w_ref[pl.ds(base + 1, step_pairs, 2), :]
        spots = (idx_ref[pl.ds(base, step_pairs, 2), :], idx_ref[pl.ds(base + 1, step_pairs, 2), :])
        made = []
        for i in range(step_pairs):
            left, right = [], []
            for which, weight in enumerate((even, odd)):
                spot = spots[which][i : i + 1]
                row = weight[i : i + 1]
                high = row.astype(BF16).astype(F32)
                kept = (row_tile == which) & (row_layer == spot // LANES)
                left.append(jnp.where(kept, jnp.where(row_high, high, row - high), 0.0))
                lane = jnp.broadcast_to((spot % LANES).astype(F32), (16, LANES)).astype(BF16)
                right.append(
                    jnp.concatenate([jnp.where(lane == lv, one, zero) for lv in level], axis=0)
                )
            out = mm_nt(
                jnp.concatenate(left, axis=1).astype(BF16), jnp.concatenate(right, axis=1)
            )
            made.append(out[:rows] + out[rows:])
        count = step_pairs * rows
        cells[pl.ds(pl.multiple_of(step * count, count), count), :] = jnp.concatenate(made, axis=0)
        return carry

    lax.fori_loop(0, steps, backward, 0)
    give = give_ref[...]
    for at in range(layers):
        high, low = split(cells[pl.ds(at, tiles, layers), :])
        grad_ref[:, at * LANES : (at + 1) * LANES] = (mm(give, high) + mm(give, low)).astype(BF16)


def shifted(values, axis):
    count = lax.axis_size(axis)
    up = [(i, i + 1) for i in range(count - 1)]
    down = [(i + 1, i) for i in range(count - 1)]
    return lax.ppermute(values, axis, up), lax.ppermute(values, axis, down)


def on_device(
    latent, observed, sigma, response, offsets, fractions, tile_group, tile_slot, send_index
):
    rows_x, rows_y, depth = latent.shape
    cells = rows_x * rows_y
    axes = ("cx", "cy")
    devices = lax.axis_size("cx") * lax.axis_size("cy")
    slots = devices * send_index.shape[2]
    tiles, samples, star_tile = response.shape
    groups = observed.shape[0] // star_tile
    own = latent.reshape(cells, depth)

    hx, hy, hz = call(
        functools.partial(operators_body, rows_x, rows_y, depth),
        [((6, cells, cells), BF16), ((6, cells, cells), BF16), ((2, depth, depth), BF16)],
        name="operators",
    )
    idx, weight, grp, take, give, pack, add_up = call(
        tables_body,
        [
            ((tiles, LANES), jnp.int32),
            ((tiles, LANES), F32),
            ((tiles // 2, LANES), jnp.int32),
            ((tiles, slots), BF16),
            ((slots, tiles), BF16),
            ((slots, cells), BF16),
            ((cells, slots), BF16),
        ],
        offsets, fractions, tile_group.reshape(1, tiles), tile_slot.reshape(1, tiles),
        send_index.reshape(1, slots),
        scratch=[pltpu.VMEM((tiles, LANES), jnp.int32)],
        name="tables",
    )
    halo = own.astype(HALO)
    before, after = shifted(halo, "cx")
    field, sent = call(
        first_body, [((cells, depth), F32), ((cells, depth), HALO)], own, before, after, hx,
        name="along_x",
    )
    before, after = shifted(sent, "cy")
    dens, packed = call(
        density_body, [((cells, depth), F32), ((slots, depth), BF16)],
        field, before, after, hy, hz, pack, name="density",
    )
    got = lax.all_to_all(packed, axes, split_axis=0, concat_axis=0, tiled=True)
    pred, grad = call(
        cone_body, [((groups, star_tile), F32), ((slots, depth), BF16)],
        got, response, idx, weight, grp, take, give,
        observed.reshape(groups, star_tile), sigma.reshape(groups, star_tile),
        scratch=[
            pltpu.VMEM((tiles, LANES), F32),
            pltpu.VMEM((tiles // 2, LANES), F32),
            pltpu.VMEM((tiles, LANES), F32),
            pltpu.VMEM((tiles * (depth // LANES), LANES), F32),
        ],
        limit=40,
        name="cones",
    )
    back = lax.all_to_all(grad, axes, split_axis=0, concat_axis=0, tiled=True)
    field, sent = call(
        owner_body, [((cells, depth), F32), ((cells, depth), BF16)], add_up, back, dens, hz,
        name="owners",
    )
    before, after = shifted(sent, "cy")
    field, sent = call(
        first_body, [((cells, depth), F32), ((cells, depth), BF16)], field, before, after, hy,
        name="along_y",
    )
    before, after = shifted(sent, "cx")
    (gradient,) = call(
        last_body, [((cells, depth), F32)], field, before, after, hx, own, name="finish"
    )
    return gradient.reshape(rows_x, rows_y, depth), pred.reshape(-1)


def solution(mesh):
    both = ("cx", "cy")
    placed = (
        P("cx", "cy", None),
        P(both),
        P(both),
        P(both, None, None),
        P(None, both),
        P(None, both),
        P(both),
        P(both),
        P(both, None, None),
    )
    return jax.shard_map(
        on_device,
        mesh=mesh,
        in_specs=placed,
        out_specs=(P("cx", "cy", None), P(both)),
        check_vma=False,
    )
```

```python
import functools
import math

import jax
import jax.numpy as jnp
from jax import lax
from jax.experimental import pallas as pl
from jax.experimental.pallas import tpu as pltpu
from jax.sharding import PartitionSpec as P

REACH = 16
LANES = 128
F32 = jnp.float32
BF16 = jnp.bfloat16
PREDICT_PAIRS = 64
BACK_PAIRS = 64


def tap_scale():
    total = 0.0
    for shift in range(-REACH, REACH + 1):
        a = math.sqrt(3.0) * abs(shift) / 8.0
        total += ((1.0 + a) * math.exp(-a)) ** 2
    return 0.8 / math.sqrt(total)


def split(values):
    high = values.astype(BF16)
    low = (values - high.astype(F32)).astype(BF16)
    return high, low


def mm(a, b):
    return jnp.dot(a, b, preferred_element_type=F32)


def mm_nt(a, b):
    return lax.dot_general(a, b, (((1,), (1,)), ((), ())), preferred_element_type=F32)


def iota(shape, dim):
    return lax.broadcasted_iota(jnp.int32, shape, dim)


def apply_left(mat_high, mat_low, values):
    if values.dtype == BF16:
        return mm(mat_high, values) + mm(mat_low, values)
    high, low = split(values)
    return mm(mat_high, high) + (mm(mat_high, low) + mm(mat_low, high))


def apply_right(values, mat_high, mat_low):
    high, low = split(values)
    return mm(high, mat_high) + (mm(low, mat_high) + mm(high, mat_low))


def call(body, outs, *args, scratch=(), limit=16, flops=0, name=None, space=pltpu.VMEM):
    shapes = [jax.ShapeDtypeStruct(s, d) for s, d in outs]
    if space is pltpu.HBM:
        args = [pltpu.with_memory_space_constraint(a, pltpu.HBM) for a in args]
    moved = sum(math.prod(a.shape) * a.dtype.itemsize for a in args) + sum(
        math.prod(s.shape) * s.dtype.itemsize for s in shapes
    )
    return pl.pallas_call(
        body,
        out_shape=shapes,
        in_specs=[pl.BlockSpec(memory_space=space)] * len(args),
        out_specs=[pl.BlockSpec(memory_space=pltpu.VMEM)] * len(shapes),
        scratch_shapes=list(scratch),
        compiler_params=pltpu.CompilerParams(vmem_limit_bytes=limit << 20),
        cost_estimate=pl.CostEstimate(flops=flops, bytes_accessed=moved, transcendentals=0),
        name=name,
    )(*args)


def taps_matrix(distance, kept):
    a = (math.sqrt(3.0) / 8.0) * jnp.abs(distance).astype(F32)
    value = (tap_scale() * (1.0 + a)) * jnp.exp(-a)
    return jnp.where(kept & (jnp.abs(distance) <= REACH), value, 0.0)


def operators(rows_x, rows_y, depth, hx_ref, hy_ref, hz_ref):
    cells = rows_x * rows_y
    out = iota((cells, cells), 0)
    inp = iota((cells, cells), 1)
    out_x, out_y = out // rows_y, out % rows_y
    inp_x, inp_y = inp // rows_y, inp % rows_y
    near_x = 2 * lax.rem(lax.axis_index("cx"), 2) - 1
    near_y = 2 * lax.rem(lax.axis_index("cy"), 2) - 1
    for at, side in enumerate((0, 1, -1)):
        high, low = split(taps_matrix(out_x - inp_x + side * near_x * rows_x, out_y == inp_y))
        hx_ref[2 * at], hx_ref[2 * at + 1] = high, low
        high, low = split(taps_matrix(out_y - inp_y + side * near_y * rows_y, out_x == inp_x))
        hy_ref[2 * at], hy_ref[2 * at + 1] = high, low
    shift = iota((depth, depth), 0) - iota((depth, depth), 1)
    high, low = split(taps_matrix(shift, shift == shift))
    hz_ref[0], hz_ref[1] = high, low


def one_hot(hits):
    return jnp.where(hits, 1.0, 0.0).astype(BF16)


def prepare_body(
    rows_x, rows_y,
    own_hbm, resp_hbm, off_hbm, frac_hbm, group_hbm, slot_hbm, send_hbm, obs_hbm, sig_hbm,
    hx_ref, hy_ref, hz_ref, part_ref, resp_ref, obs_ref, var_ref,
    idx_ref, w_ref, grp_ref, take_ref, give_ref, pack_ref, sum_ref,
    own_ref, off_ref, frac_ref, group_ref, slot_ref, send_ref, sig_ref, keep, sems,
):
    moves = (
        (own_hbm, own_ref), (off_hbm, off_ref), (frac_hbm, frac_ref), (group_hbm, group_ref),
        (slot_hbm, slot_ref), (send_hbm, send_ref), (obs_hbm, obs_ref), (sig_hbm, sig_ref),
        (resp_hbm, resp_ref),
    )
    copies = [
        pltpu.make_async_copy(src, dst, sems.at[at]) for at, (src, dst) in enumerate(moves)
    ]
    for copy in copies:
        copy.start()
    operators(rows_x, rows_y, hz_ref.shape[1], hx_ref, hy_ref, hz_ref)
    for copy in copies[:-1]:
        copy.wait()
    part_ref[...] = apply_left(hx_ref[0], hx_ref[1], own_ref[...])
    sig = sig_ref[...]
    var_ref[...] = sig * sig
    tiles = off_ref.shape[1]
    slots = take_ref.shape[1]
    cells = pack_ref.shape[1]
    off = off_ref[...]
    frac = frac_ref[...]
    idx_ref[...] = jnp.concatenate([off, off + 1], axis=0).T
    w_ref[...] = jnp.concatenate([1.0 - frac, frac], axis=0).T
    keep[...] = jnp.broadcast_to(group_ref[...], (LANES, tiles)).T
    first = iota((tiles // 2, LANES), 1) < LANES // 2
    grp_ref[...] = jnp.where(
        first, keep[pl.ds(0, tiles // 2, 2), :], keep[pl.ds(1, tiles // 2, 2), :]
    )
    slot = slot_ref[...]
    wide = jnp.broadcast_to(slot, (LANES, tiles)).T
    for at in range(0, slots, LANES):
        take_ref[:, at : at + LANES] = one_hot(wide == iota((tiles, LANES), 1) + at)
    give_ref[...] = one_hot(jnp.broadcast_to(slot, (slots, tiles)) == iota((slots, tiles), 0))
    send = send_ref[...]
    wide = jnp.broadcast_to(send, (LANES, slots)).T
    for at in range(0, cells, LANES):
        pack_ref[:, at : at + LANES] = one_hot(wide == iota((slots, LANES), 1) + at)
    sum_ref[...] = one_hot(jnp.broadcast_to(send, (cells, slots)) == iota((cells, slots), 0))
    copies[-1].wait()


def sides(mats_ref, near, far):
    return apply_left(mats_ref[2], mats_ref[3], near) + apply_left(mats_ref[4], mats_ref[5], far)


def three(mats_ref, own, near, far):
    return apply_left(mats_ref[0], mats_ref[1], own) + sides(mats_ref, near, far)


def join_body(part_ref, near_ref, far_ref, mats_ref, out_ref, sent_ref):
    out = part_ref[...] + sides(mats_ref, near_ref[...], far_ref[...])
    out_ref[...] = out
    sent_ref[...] = out.astype(sent_ref.dtype)


def smooth_body(own_ref, near_ref, far_ref, mats_ref, out_ref, sent_ref):
    out = three(mats_ref, own_ref[...], near_ref[...], far_ref[...])
    out_ref[...] = out
    sent_ref[...] = out.astype(sent_ref.dtype)


def density_body(own_ref, near_ref, far_ref, mats_ref, hz_ref, pack_ref, dens_ref, packed_ref):
    out = three(mats_ref, own_ref[...], near_ref[...], far_ref[...])
    dens = jnp.exp(apply_right(out, hz_ref[0], hz_ref[1]))
    dens_ref[...] = dens
    packed_ref[...] = mm(pack_ref[...], dens.astype(BF16)).astype(BF16)


def owner_body(sum_ref, back_ref, dens_ref, hz_ref, out_ref, sent_ref):
    grad = dens_ref[...] * mm(sum_ref[...], back_ref[...])
    out = apply_right(grad, hz_ref[0], hz_ref[1])
    out_ref[...] = out
    sent_ref[...] = out.astype(sent_ref.dtype)


def last_body(own_ref, near_ref, far_ref, mats_ref, latent_ref, out_ref):
    out_ref[...] = latent_ref[...] + three(mats_ref, own_ref[...], near_ref[...], far_ref[...])


def cone_body(
    got_ref, resp_ref, idx_ref, w_ref, grp_ref, take_ref, give_ref, obs_ref, var_ref,
    pred_ref, grad_ref, both, pairs, cells,
):
    tiles, samples, star_tile = resp_ref.shape
    depth = got_ref.shape[1]
    groups = obs_ref.shape[0]
    half = LANES // 2
    layers = depth // LANES
    idx = idx_ref[...]
    columns = mm(take_ref[...], got_ref[...])
    value = jnp.zeros((tiles, LANES), F32)
    for at in range(layers):
        piece = jnp.take_along_axis(columns[:, at * LANES : (at + 1) * LANES], idx % LANES, axis=1)
        value = jnp.where(idx // LANES == at, piece, value)
    value = w_ref[...] * value
    both[...] = value + pltpu.roll(value, half, 1)
    first = iota((tiles // 2, LANES), 1) < half
    pairs[...] = jnp.where(
        first, both[pl.ds(0, tiles // 2, 2), :], both[pl.ds(1, tiles // 2, 2), :]
    )
    group_at = iota((groups, LANES), 0)

    def rows_of(ref, step, count):
        return ref[pl.ds(pl.multiple_of(step * count, count), count)].reshape(
            count * samples, star_tile
        )

    def pair_rows(ref, step, count):
        return ref[pl.ds(pl.multiple_of(step * count, count), count), :]

    def predict(step, total):
        pair = pair_rows(pairs, step, PREDICT_PAIRS)
        group = pair_rows(grp_ref, step, PREDICT_PAIRS)
        left = [
            jnp.where(group[i : i + 1] == group_at, pair[i : i + 1], 0.0)
            for i in range(PREDICT_PAIRS)
        ]
        left = jnp.concatenate(left, axis=1).astype(BF16)
        return total + mm(left, rows_of(resp_ref, step, 2 * PREDICT_PAIRS))

    pred = lax.fori_loop(
        0, tiles // (2 * PREDICT_PAIRS), predict, jnp.zeros((groups, star_tile), F32)
    )
    pred_ref[...] = pred
    resid = ((pred - obs_ref[...]) / var_ref[...]).astype(BF16)
    rows = 2 * layers
    at_row = iota((2 * rows, LANES), 0)
    row_layer = at_row % layers
    row_tile = (at_row % rows) // layers
    row_high = at_row < rows
    level = [(iota((16, LANES), 0) + 16 * k).astype(F32).astype(BF16) for k in range(LANES // 16)]
    one = jnp.ones((16, LANES), BF16)
    zero = jnp.zeros((16, LANES), BF16)

    step_pairs = BACK_PAIRS
    step_tiles = 2 * step_pairs
    lane_first = iota((step_pairs, LANES), 1) < half

    def backward(step, carry):
        group = pair_rows(grp_ref, step, step_pairs)
        back = mm_nt(resid, rows_of(resp_ref, step, step_tiles))
        picked = [
            jnp.sum(
                jnp.where(group[i : i + 1] == group_at, back[:, i * LANES : (i + 1) * LANES], 0.0),
                axis=0, keepdims=True,
            )
            for i in range(step_pairs)
        ]
        picked = jnp.concatenate(picked, axis=0)
        swapped = pltpu.roll(picked, half, 1)
        base = pl.multiple_of(step * step_tiles, step_tiles)
        even = jnp.where(lane_first, picked, swapped) * w_ref[pl.ds(base, step_pairs, 2), :]
        odd = jnp.where(lane_first, swapped, picked) * w_ref[pl.ds(base + 1, step_pairs, 2), :]
        spots = (idx_ref[pl.ds(base, step_pairs, 2), :], idx_ref[pl.ds(base + 1, step_pairs, 2), :])
        made = []
        for i in range(step_pairs):
            left, right = [], []
            for which, weight in enumerate((even, odd)):
                spot = spots[which][i : i + 1]
                row = weight[i : i + 1]
                high = row.astype(BF16).astype(F32)
                kept = (row_tile == which) & (row_layer == spot // LANES)
                left.append(jnp.where(kept, jnp.where(row_high, high, row - high), 0.0))
                lane = jnp.broadcast_to((spot % LANES).astype(F32), (16, LANES)).astype(BF16)
                right.append(
                    jnp.concatenate([jnp.where(lane == lv, one, zero) for lv in level], axis=0)
                )
            out = mm_nt(
                jnp.concatenate(left, axis=1).astype(BF16), jnp.concatenate(right, axis=1)
            )
            made.append(out[:rows] + out[rows:])
        count = step_pairs * rows
        cells[pl.ds(pl.multiple_of(step * count, count), count), :] = jnp.concatenate(made, axis=0)
        return carry

    lax.fori_loop(0, tiles // step_tiles, backward, 0)
    give = give_ref[...]
    for at in range(layers):
        high, low = split(cells[pl.ds(at, tiles, layers), :])
        grad_ref[:, at * LANES : (at + 1) * LANES] = (mm(give, high) + mm(give, low)).astype(BF16)


def exchanged(values, axis):
    count = lax.axis_size(axis)
    return [
        lax.ppermute(
            values, axis,
            [pair for i in range(first, count - 1, 2) for pair in ((i, i + 1), (i + 1, i))],
        )
        for first in (0, 1)
    ]


def on_device(
    latent, observed, sigma, response, offsets, fractions, tile_group, tile_slot, send_index
):
    rows_x, rows_y, depth = latent.shape
    cells = rows_x * rows_y
    axes = ("cx", "cy")
    devices = lax.axis_size("cx") * lax.axis_size("cy")
    slots = devices * send_index.shape[2]
    tiles, samples, star_tile = response.shape
    groups = observed.shape[0] // star_tile
    own = latent.reshape(cells, depth)
    field_out = ((cells, depth), F32)
    sent_out = ((cells, depth), BF16)

    near, far = exchanged(own.astype(BF16), "cx")
    hx, hy, hz, part, resp, obs, var, idx, weight, grp, take, give, pack, add_up = call(
        functools.partial(prepare_body, rows_x, rows_y),
        [
            ((6, cells, cells), BF16),
            ((6, cells, cells), BF16),
            ((2, depth, depth), BF16),
            field_out,
            (response.shape, BF16),
            ((groups, star_tile), F32),
            ((groups, star_tile), F32),
            ((tiles, LANES), jnp.int32),
            ((tiles, LANES), F32),
            ((tiles // 2, LANES), jnp.int32),
            ((tiles, slots), BF16),
            ((slots, tiles), BF16),
            ((slots, cells), BF16),
            ((cells, slots), BF16),
        ],
        own, response, offsets, fractions,
        tile_group.reshape(1, tiles), tile_slot.reshape(1, tiles), send_index.reshape(1, slots),
        observed.reshape(groups, star_tile), sigma.reshape(groups, star_tile),
        scratch=[
            pltpu.VMEM((cells, depth), F32),
            pltpu.VMEM((samples, tiles), jnp.int32),
            pltpu.VMEM((samples, tiles), F32),
            pltpu.VMEM((1, tiles), jnp.int32),
            pltpu.VMEM((1, tiles), jnp.int32),
            pltpu.VMEM((1, slots), jnp.int32),
            pltpu.VMEM((groups, star_tile), F32),
            pltpu.VMEM((tiles, LANES), jnp.int32),
            pltpu.SemaphoreType.DMA((9,)),
        ],
        limit=20,
        space=pltpu.HBM,
        name="prepare",
    )
    field, sent = call(join_body, [field_out, sent_out], part, near, far, hx, name="along_x")
    near, far = exchanged(sent, "cy")
    dens, packed = call(
        density_body, [field_out, ((slots, depth), BF16)],
        field, near, far, hy, hz, pack, name="density",
    )
    got = lax.all_to_all(packed, axes, split_axis=0, concat_axis=0, tiled=True)
    pred, grad = call(
        cone_body, [((groups, star_tile), F32), ((slots, depth), BF16)],
        got, resp, idx, weight, grp, take, give, obs, var,
        scratch=[
            pltpu.VMEM((tiles, LANES), F32),
            pltpu.VMEM((tiles // 2, LANES), F32),
            pltpu.VMEM((tiles * (depth // LANES), LANES), F32),
        ],
        limit=20,
        name="cones",
    )
    back = lax.all_to_all(grad, axes, split_axis=0, concat_axis=0, tiled=True)
    field, sent = call(owner_body, [field_out, sent_out], add_up, back, dens, hz, name="owners")
    near, far = exchanged(sent, "cy")
    field, sent = call(
        smooth_body, [field_out, sent_out], field, near, far, hy, name="along_y"
    )
    near, far = exchanged(sent, "cx")
    (gradient,) = call(last_body, [field_out], field, near, far, hx, own, name="finish")
    return gradient.reshape(rows_x, rows_y, depth), pred.reshape(-1)


def solution(mesh):
    both = ("cx", "cy")
    placed = (
        P("cx", "cy", None),
        P(both),
        P(both),
        P(both, None, None),
        P(None, both),
        P(None, both),
        P(both),
        P(both),
        P(both, None, None),
    )
    return jax.shard_map(
        on_device,
        mesh=mesh,
        in_specs=placed,
        out_specs=(P("cx", "cy", None), P(both)),
        check_vma=False,
    )
```

```python
import functools
import math

import jax
import jax.numpy as jnp
from jax import lax
from jax.experimental import pallas as pl
from jax.experimental.pallas import tpu as pltpu
from jax.sharding import PartitionSpec as P

REACH = 16
LANES = 128
F32 = jnp.float32
BF16 = jnp.bfloat16
PREDICT_PAIRS = 64
BACK_PAIRS = 64
PART = 64


def tap_scale():
    total = 0.0
    for shift in range(-REACH, REACH + 1):
        a = math.sqrt(3.0) * abs(shift) / 8.0
        total += ((1.0 + a) * math.exp(-a)) ** 2
    return 0.8 / math.sqrt(total)


def split(values):
    high = values.astype(BF16)
    low = (values - high.astype(F32)).astype(BF16)
    return high, low


def mm(a, b):
    return jnp.dot(a, b, preferred_element_type=F32)


def mm_nt(a, b):
    return lax.dot_general(a, b, (((1,), (1,)), ((), ())), preferred_element_type=F32)


def iota(shape, dim):
    return lax.broadcasted_iota(jnp.int32, shape, dim)


def apply_left(mat_high, mat_low, values):
    if values.dtype == BF16:
        return mm(mat_high, values) + mm(mat_low, values)
    high, low = split(values)
    return mm(mat_high, high) + (mm(mat_high, low) + mm(mat_low, high))


def apply_right(values, mat_high, mat_low):
    high, low = split(values)
    return mm(high, mat_high) + (mm(low, mat_high) + mm(high, mat_low))


def hbm(array):
    return pltpu.with_memory_space_constraint(array, pltpu.HBM)


def is_hbm(array):
    return getattr(jax.typeof(array), "memory_space", None) is pltpu.HBM


def call(body, outs, *args, scratch=(), limit=16, name=None):
    shapes = [jax.ShapeDtypeStruct(s, d) for s, d in outs]
    moved = sum(math.prod(a.shape) * a.dtype.itemsize for a in args) + sum(
        math.prod(s.shape) * s.dtype.itemsize for s in shapes
    )
    return pl.pallas_call(
        body,
        out_shape=shapes,
        in_specs=[
            pl.BlockSpec(memory_space=pltpu.HBM if is_hbm(a) else pltpu.VMEM) for a in args
        ],
        out_specs=[pl.BlockSpec(memory_space=pltpu.VMEM)] * len(shapes),
        scratch_shapes=list(scratch),
        compiler_params=pltpu.CompilerParams(vmem_limit_bytes=limit << 20),
        cost_estimate=pl.CostEstimate(flops=0, bytes_accessed=moved, transcendentals=0),
        name=name,
    )(*args)


def taps_matrix(distance, kept):
    a = (math.sqrt(3.0) / 8.0) * jnp.abs(distance).astype(F32)
    value = (tap_scale() * (1.0 + a)) * jnp.exp(-a)
    return jnp.where(kept & (jnp.abs(distance) <= REACH), value, 0.0)


def operators(rows_x, rows_y, depth, hx_ref, hy_ref, hz_ref):
    cells = rows_x * rows_y
    out = iota((cells, cells), 0)
    inp = iota((cells, cells), 1)
    out_x, out_y = out // rows_y, out % rows_y
    inp_x, inp_y = inp // rows_y, inp % rows_y
    near_x = 2 * lax.rem(lax.axis_index("cx"), 2) - 1
    near_y = 2 * lax.rem(lax.axis_index("cy"), 2) - 1
    for at, side in enumerate((0, 1, -1)):
        high, low = split(taps_matrix(out_x - inp_x + side * near_x * rows_x, out_y == inp_y))
        hx_ref[2 * at], hx_ref[2 * at + 1] = high, low
        high, low = split(taps_matrix(out_y - inp_y + side * near_y * rows_y, out_x == inp_x))
        hy_ref[2 * at], hy_ref[2 * at + 1] = high, low
    shift = iota((depth, depth), 0) - iota((depth, depth), 1)
    high, low = split(taps_matrix(shift, shift == shift))
    hz_ref[0], hz_ref[1] = high, low


def one_hot(hits):
    return jnp.where(hits, 1.0, 0.0).astype(BF16)


def fetch(moves, sems):
    copies = [
        pltpu.make_async_copy(src, dst, sems.at[at]) for at, (src, dst) in enumerate(moves)
    ]
    for copy in copies:
        copy.start()
    return copies


def operators_body(
    rows_x, rows_y, own_hbm, resp_hbm, after_hbm,
    hx_ref, hy_ref, hz_ref, part_ref, resp_ref, own_ref, sems,
):
    count = resp_ref.shape[0]
    copies = fetch([(own_hbm, own_ref), (resp_hbm.at[pl.ds(0, count)], resp_ref)], sems)
    operators(rows_x, rows_y, hz_ref.shape[1], hx_ref, hy_ref, hz_ref)
    copies[0].wait()
    part_ref[...] = apply_left(hx_ref[0], hx_ref[1], own_ref[...])
    copies[1].wait()


def tables_body(
    off_hbm, frac_hbm, group_hbm, slot_hbm, send_hbm, obs_hbm, sig_hbm, resp_hbm,
    field_ref, hy_ref, hz_ref,
    part_ref, resp_ref, obs_ref, var_ref, idx_ref, w_ref, grp_ref, take_ref, give_ref, pack_ref, sum_ref,
    off_ref, frac_ref, group_ref, slot_ref, send_ref, sig_ref, keep, sems,
):
    count = resp_ref.shape[0]
    copies = fetch(
        [
            (send_hbm, send_ref), (slot_hbm, slot_ref), (group_hbm, group_ref),
            (off_hbm, off_ref), (frac_hbm, frac_ref), (obs_hbm, obs_ref), (sig_hbm, sig_ref),
            (resp_hbm.at[pl.ds(resp_hbm.shape[0] - count, count)], resp_ref),
        ],
        sems,
    )
    part = apply_left(hy_ref[0], hy_ref[1], field_ref[...])
    part_ref[...] = apply_right(part, hz_ref[0], hz_ref[1])
    for copy in copies[:-1]:
        copy.wait()
    sig = sig_ref[...]
    var_ref[...] = sig * sig
    tiles = off_ref.shape[1]
    slots = take_ref.shape[1]
    cells = pack_ref.shape[1]
    off = off_ref[...]
    frac = frac_ref[...]
    idx_ref[...] = jnp.concatenate([off, off + 1], axis=0).T
    w_ref[...] = jnp.concatenate([1.0 - frac, frac], axis=0).T
    keep[...] = jnp.broadcast_to(group_ref[...], (LANES, tiles)).T
    first = iota((tiles // 2, LANES), 1) < LANES // 2
    grp_ref[...] = jnp.where(
        first, keep[pl.ds(0, tiles // 2, 2), :], keep[pl.ds(1, tiles // 2, 2), :]
    )
    slot = slot_ref[...]
    wide = jnp.broadcast_to(slot, (LANES, tiles)).T
    for at in range(0, slots, LANES):
        take_ref[:, at : at + LANES] = one_hot(wide == iota((tiles, LANES), 1) + at)
    give_ref[...] = one_hot(jnp.broadcast_to(slot, (slots, tiles)) == iota((slots, tiles), 0))
    send = send_ref[...]
    wide = jnp.broadcast_to(send, (LANES, slots)).T
    for at in range(0, cells, LANES):
        pack_ref[:, at : at + LANES] = one_hot(wide == iota((slots, LANES), 1) + at)
    sum_ref[...] = one_hot(jnp.broadcast_to(send, (cells, slots)) == iota((cells, slots), 0))
    copies[-1].wait()


def sides(mats_ref, near, far):
    return apply_left(mats_ref[2], mats_ref[3], near) + apply_left(mats_ref[4], mats_ref[5], far)


def own_body(own_ref, mats_ref, part_ref):
    part_ref[...] = apply_left(mats_ref[0], mats_ref[1], own_ref[...])


def own_latent_body(own_ref, mats_ref, latent_ref, part_ref):
    part_ref[...] = latent_ref[...] + apply_left(mats_ref[0], mats_ref[1], own_ref[...])


def join_body(part_ref, near_ref, far_ref, mats_ref, out_ref, *sent_ref):
    out = part_ref[...] + sides(mats_ref, near_ref[...], far_ref[...])
    out_ref[...] = out
    for ref in sent_ref:
        ref[...] = out.astype(ref.dtype)


def density_body(part_ref, near_ref, far_ref, mats_ref, hz_ref, pack_ref, dens_ref, packed_ref):
    out = sides(mats_ref, near_ref[...], far_ref[...])
    dens = jnp.exp(part_ref[...] + apply_right(out, hz_ref[0], hz_ref[1]))
    dens_ref[...] = dens
    packed_ref[...] = mm(pack_ref[...], dens.astype(BF16)).astype(BF16)


def owner_body(sum_ref, back_ref, dens_ref, hz_ref, out_ref, sent_ref):
    grad = dens_ref[...] * mm(sum_ref[...], back_ref[...])
    out = apply_right(grad, hz_ref[0], hz_ref[1])
    out_ref[...] = out
    sent_ref[...] = out.astype(sent_ref.dtype)


def cone_body(
    got_ref, early_ref, late_ref, idx_ref, w_ref, grp_ref, take_ref, give_ref, obs_ref, var_ref,
    pred_ref, grad_ref, both, pairs, cells,
):
    early, samples, star_tile = early_ref.shape
    tiles = idx_ref.shape[0]
    depth = got_ref.shape[1]
    groups = obs_ref.shape[0]
    half = LANES // 2
    idx = idx_ref[...]
    columns = mm(take_ref[...], got_ref[...])
    value = jnp.zeros((tiles, LANES), F32)
    for at in range(0, depth, LANES):
        piece = jnp.take_along_axis(columns[:, at : at + LANES], idx & (LANES - 1), axis=1)
        value = jnp.where((idx >= at) & (idx < at + LANES), piece, value) if at else piece
    value = w_ref[...] * value
    both[...] = value + pltpu.roll(value, half, 1)
    first = iota((tiles // 2, LANES), 1) < half
    pairs[...] = jnp.where(
        first, both[pl.ds(0, tiles // 2, 2), :], both[pl.ds(1, tiles // 2, 2), :]
    )
    group_at = iota((groups, LANES), 0)

    def pair_rows(ref, step, count):
        return ref[pl.ds(pl.multiple_of(step * count, count), count), :]

    def rays(ref, step, count):
        rows = ref[pl.ds(pl.multiple_of(step * count, count), count)]
        return rows.reshape(count * samples, star_tile)

    def predict(ref, before, step, total):
        pair = pair_rows(pairs, step + before, PREDICT_PAIRS)
        group = pair_rows(grp_ref, step + before, PREDICT_PAIRS)
        left = [
            jnp.where(group[i : i + 1] == group_at, pair[i : i + 1], 0.0)
            for i in range(PREDICT_PAIRS)
        ]
        left = jnp.concatenate(left, axis=1).astype(BF16)
        return total + mm(left, rays(ref, step, 2 * PREDICT_PAIRS))

    count = 2 * PREDICT_PAIRS
    pred = jnp.zeros((groups, star_tile), F32)
    for ref, before in ((early_ref, 0), (late_ref, early)):
        pred = lax.fori_loop(
            0, ref.shape[0] // count, functools.partial(predict, ref, before // count), pred
        )
    pred_ref[...] = pred
    resid = ((pred - obs_ref[...]) / var_ref[...]).astype(BF16)
    parts = depth // PART
    rows = 2 * parts
    at_row = iota((2 * rows, LANES), 0)
    row_part = at_row & (parts - 1)
    row_second = (at_row & parts) != 0
    row_high = at_row < rows
    level = [(iota((16, LANES), 0) + at).astype(F32).astype(BF16) for at in range(0, PART, 16)]
    one = jnp.ones((16, LANES), BF16)
    zero = jnp.zeros((16, LANES), BF16)
    step_pairs = BACK_PAIRS
    step_tiles = 2 * step_pairs
    lane_first = iota((step_pairs, LANES), 1) < half

    def backward(ref, before, step, carry):
        back = mm_nt(resid, rays(ref, step, step_tiles))
        step = step + before
        group = pair_rows(grp_ref, step, step_pairs)
        picked = [
            jnp.sum(
                jnp.where(group[i : i + 1] == group_at, back[:, i * LANES : (i + 1) * LANES], 0.0),
                axis=0, keepdims=True,
            )
            for i in range(step_pairs)
        ]
        picked = jnp.concatenate(picked, axis=0)
        swapped = pltpu.roll(picked, half, 1)
        base = pl.multiple_of(step * step_tiles, step_tiles)
        even, odd = pl.ds(base, step_pairs, 2), pl.ds(base + 1, step_pairs, 2)
        weights = (
            jnp.where(lane_first, picked, swapped) * w_ref[even, :],
            jnp.where(lane_first, swapped, picked) * w_ref[odd, :],
        )
        highs = [weight.astype(BF16).astype(F32) for weight in weights]
        lows = [weight - high for weight, high in zip(weights, highs)]
        spots = (idx_ref[even, :], idx_ref[odd, :])
        lanes = [(spot & (PART - 1)).astype(F32) for spot in spots]
        shift = PART.bit_length() - 1
        blocks = [lax.shift_right_logical(spot, shift) for spot in spots]
        made = []
        for i in range(step_pairs):
            left, right = [], []
            for which in (0, 1):
                block = blocks[which][i : i + 1]
                kept = (row_second == bool(which)) & (row_part == block)
                both_parts = jnp.where(
                    row_high, highs[which][i : i + 1], lows[which][i : i + 1]
                )
                left.append(jnp.where(kept, both_parts, 0.0))
                lane = jnp.broadcast_to(lanes[which][i : i + 1], (16, LANES)).astype(BF16)
                right.append(
                    jnp.concatenate([jnp.where(lane == lv, one, zero) for lv in level], axis=0)
                )
            out = mm_nt(
                jnp.concatenate(left, axis=1).astype(BF16), jnp.concatenate(right, axis=1)
            )
            made.append(out[:rows] + out[rows:])
        count = step_pairs * rows
        cells[pl.ds(pl.multiple_of(step * count, count), count), :] = jnp.concatenate(made, axis=0)
        return carry

    for ref, before in ((early_ref, 0), (late_ref, early)):
        steps = ref.shape[0] // step_tiles
        lax.fori_loop(0, steps, functools.partial(backward, ref, before // step_tiles), 0)
    give = give_ref[...]
    for at in range(0, depth, LANES):
        pieces = [
            cells[pl.ds(part, tiles, parts), :]
            for part in range(at // PART, (at + LANES) // PART)
        ]
        high, low = split(jnp.concatenate(pieces, axis=1))
        grad_ref[:, at : at + LANES] = (mm(give, high) + mm(give, low)).astype(BF16)


def exchanged(values, axis):
    count = lax.axis_size(axis)
    return [
        lax.ppermute(
            values, axis,
            [pair for i in range(first, count - 1, 2) for pair in ((i, i + 1), (i + 1, i))],
        )
        for first in (0, 1)
    ]


def on_device(
    latent, observed, sigma, response, offsets, fractions, tile_group, tile_slot, send_index
):
    rows_x, rows_y, depth = latent.shape
    cells = rows_x * rows_y
    axes = ("cx", "cy")
    devices = lax.axis_size("cx") * lax.axis_size("cy")
    slots = devices * send_index.shape[2]
    tiles, samples, star_tile = response.shape
    groups = observed.shape[0] // star_tile
    own = latent.reshape(cells, depth)
    field_out = ((cells, depth), F32)
    sent_out = ((cells, depth), BF16)

    send = send_index.reshape(1, slots)
    ray_out = ((tiles // 2, samples, star_tile), BF16)
    near, far = exchanged(own.astype(BF16), "cx")
    hx, hy, hz, part, early = call(
        functools.partial(operators_body, rows_x, rows_y),
        [
            ((6, cells, cells), BF16), ((6, cells, cells), BF16), ((2, depth, depth), BF16),
            field_out, ray_out,
        ],
        hbm(own), hbm(response), hbm(send),
        scratch=[pltpu.VMEM((cells, depth), F32), pltpu.SemaphoreType.DMA((2,))],
        name="operators",
    )
    field, sent = call(join_body, [field_out, sent_out], part, near, far, hx, name="along_x")
    near, far = exchanged(sent, "cy")
    part, late, obs, var, idx, weight, grp, take, give, pack, add_up = call(
        tables_body,
        [
            field_out,
            ray_out,
            ((groups, star_tile), F32),
            ((groups, star_tile), F32),
            ((tiles, LANES), jnp.int32),
            ((tiles, LANES), F32),
            ((tiles // 2, LANES), jnp.int32),
            ((tiles, slots), BF16),
            ((slots, tiles), BF16),
            ((slots, cells), BF16),
            ((cells, slots), BF16),
        ],
        hbm(offsets), hbm(fractions), hbm(tile_group.reshape(1, tiles)),
        hbm(tile_slot.reshape(1, tiles)), hbm(send),
        hbm(observed.reshape(groups, star_tile)), hbm(sigma.reshape(groups, star_tile)),
        hbm(response), field, hy, hz,
        scratch=[
            pltpu.VMEM((samples, tiles), jnp.int32),
            pltpu.VMEM((samples, tiles), F32),
            pltpu.VMEM((1, tiles), jnp.int32),
            pltpu.VMEM((1, tiles), jnp.int32),
            pltpu.VMEM((1, slots), jnp.int32),
            pltpu.VMEM((groups, star_tile), F32),
            pltpu.VMEM((tiles, LANES), jnp.int32),
            pltpu.SemaphoreType.DMA((8,)),
        ],
        name="tables",
    )
    dens, packed = call(
        density_body, [field_out, ((slots, depth), BF16)],
        part, near, far, hy, hz, pack, name="density",
    )
    got = lax.all_to_all(packed, axes, split_axis=0, concat_axis=0, tiled=True)
    pred, grad = call(
        cone_body, [((groups, star_tile), F32), ((slots, depth), BF16)],
        got, early, late, idx, weight, grp, take, give, obs, var,
        scratch=[
            pltpu.VMEM((tiles, LANES), F32),
            pltpu.VMEM((tiles // 2, LANES), F32),
            pltpu.VMEM((tiles * (depth // PART), PART), F32),
        ],
        limit=20,
        name="cones",
    )
    back = lax.all_to_all(grad, axes, split_axis=0, concat_axis=0, tiled=True)
    field, sent = call(owner_body, [field_out, sent_out], add_up, back, dens, hz, name="owners")
    near, far = exchanged(sent, "cy")
    (part,) = call(own_body, [field_out], field, hy, name="own_y")
    field, sent = call(join_body, [field_out, sent_out], part, near, far, hy, name="along_y")
    near, far = exchanged(sent, "cx")
    (part,) = call(own_latent_body, [field_out], field, hx, own, name="own_x")
    (gradient,) = call(join_body, [field_out], part, near, far, hx, name="finish")
    return gradient.reshape(rows_x, rows_y, depth), pred.reshape(-1)


def solution(mesh):
    both = ("cx", "cy")
    placed = (
        P("cx", "cy", None),
        P(both),
        P(both),
        P(both, None, None),
        P(None, both),
        P(None, both),
        P(both),
        P(both),
        P(both, None, None),
    )
    return jax.shard_map(
        on_device,
        mesh=mesh,
        in_specs=placed,
        out_specs=(P("cx", "cy", None), P(both)),
        check_vma=False,
    )
```

```python
import functools
import math

import jax
import jax.numpy as jnp
from jax import lax
from jax.experimental import pallas as pl
from jax.experimental.pallas import tpu as pltpu
from jax.sharding import PartitionSpec as P

REACH = 16
LANES = 128
F32 = jnp.float32
BF16 = jnp.bfloat16
AHEAD = 256
CHUNK = 256
GIVE = 256
PART = 32


def tap_scale():
    total = 0.0
    for shift in range(-REACH, REACH + 1):
        a = math.sqrt(3.0) * abs(shift) / 8.0
        total += ((1.0 + a) * math.exp(-a)) ** 2
    return 0.8 / math.sqrt(total)


def split(values):
    high = values.astype(BF16)
    low = (values - high.astype(F32)).astype(BF16)
    return high, low


def mm(a, b):
    return jnp.dot(a, b, preferred_element_type=F32)


def mm_nt(a, b):
    return lax.dot_general(a, b, (((1,), (1,)), ((), ())), preferred_element_type=F32)


def iota(shape, dim):
    return lax.broadcasted_iota(jnp.int32, shape, dim)


def apply_left(mat_high, mat_low, values):
    if values.dtype == BF16:
        return mm(mat_high, values) + mm(mat_low, values)
    high, low = split(values)
    return mm(mat_high, high) + (mm(mat_high, low) + mm(mat_low, high))


def apply_right(values, mat_high, mat_low):
    high, low = split(values)
    return mm(high, mat_high) + (mm(low, mat_high) + mm(high, mat_low))


def hbm(array):
    return pltpu.with_memory_space_constraint(array, pltpu.HBM)


def is_hbm(array):
    return getattr(jax.typeof(array), "memory_space", None) is pltpu.HBM


def call(body, outs, *args, scratch=(), limit=16, name=None):
    shapes = [jax.ShapeDtypeStruct(s, d) for s, d in outs]
    moved = sum(math.prod(a.shape) * a.dtype.itemsize for a in args) + sum(
        math.prod(s.shape) * s.dtype.itemsize for s in shapes
    )
    return pl.pallas_call(
        body,
        out_shape=shapes,
        in_specs=[
            pl.BlockSpec(memory_space=pltpu.HBM if is_hbm(a) else pltpu.VMEM) for a in args
        ],
        out_specs=[pl.BlockSpec(memory_space=pltpu.VMEM)] * len(shapes),
        scratch_shapes=list(scratch),
        compiler_params=pltpu.CompilerParams(vmem_limit_bytes=limit << 20),
        cost_estimate=pl.CostEstimate(flops=0, bytes_accessed=moved, transcendentals=0),
        name=name,
    )(*args)


def taps_matrix(distance, kept):
    a = (math.sqrt(3.0) / 8.0) * jnp.abs(distance).astype(F32)
    value = (tap_scale() * (1.0 + a)) * jnp.exp(-a)
    return jnp.where(kept & (jnp.abs(distance) <= REACH), value, 0.0)


def operators(rows_x, rows_y, depth, hx_ref, hy_ref, hz_ref):
    cells = rows_x * rows_y
    out = iota((cells, cells), 0)
    inp = iota((cells, cells), 1)
    out_x, out_y = out // rows_y, out % rows_y
    inp_x, inp_y = inp // rows_y, inp % rows_y
    near_x = 2 * lax.rem(lax.axis_index("cx"), 2) - 1
    near_y = 2 * lax.rem(lax.axis_index("cy"), 2) - 1
    for at, side in enumerate((0, 1, -1)):
        high, low = split(taps_matrix(out_x - inp_x + side * near_x * rows_x, out_y == inp_y))
        hx_ref[2 * at], hx_ref[2 * at + 1] = high, low
        high, low = split(taps_matrix(out_y - inp_y + side * near_y * rows_y, out_x == inp_x))
        hy_ref[2 * at], hy_ref[2 * at + 1] = high, low
    shift = iota((depth, depth), 0) - iota((depth, depth), 1)
    high, low = split(taps_matrix(shift, shift == shift))
    hz_ref[0], hz_ref[1] = high, low


def one_hot(hits):
    return jnp.where(hits, 1.0, 0.0).astype(BF16)


def fetch(moves, sems):
    copies = [
        pltpu.make_async_copy(src, dst, sems.at[at]) for at, (src, dst) in enumerate(moves)
    ]
    for copy in copies:
        copy.start()
    return copies


def operators_body(
    rows_x, rows_y, own_hbm, resp_hbm, after_hbm,
    hx_ref, hy_ref, hz_ref, part_ref, resp_ref, own_ref, sems,
):
    count = resp_ref.shape[0]
    copies = fetch([(own_hbm, own_ref), (resp_hbm.at[pl.ds(0, count)], resp_ref)], sems)
    operators(rows_x, rows_y, hz_ref.shape[1], hx_ref, hy_ref, hz_ref)
    copies[0].wait()
    part_ref[...] = apply_left(hx_ref[0], hx_ref[1], own_ref[...])
    copies[1].wait()


def tables_body(
    off_hbm, frac_hbm, group_hbm, slot_hbm, send_hbm, obs_hbm, sig_hbm, resp_hbm,
    field_ref, hy_ref, hz_ref,
    part_ref, resp_ref, obs_ref, var_ref, idx_ref, w_ref, grp_ref, take_ref, give_ref, pack_ref, sum_ref,
    off_ref, frac_ref, group_ref, slot_ref, send_ref, sig_ref, keep, sems,
):
    count = resp_ref.shape[0]
    copies = fetch(
        [
            (send_hbm, send_ref), (slot_hbm, slot_ref), (group_hbm, group_ref),
            (off_hbm, off_ref), (frac_hbm, frac_ref), (obs_hbm, obs_ref), (sig_hbm, sig_ref),
            (resp_hbm.at[pl.ds(resp_hbm.shape[0] - count, count)], resp_ref),
        ],
        sems,
    )
    part = apply_left(hy_ref[0], hy_ref[1], field_ref[...])
    part_ref[...] = apply_right(part, hz_ref[0], hz_ref[1])
    for copy in copies[:-1]:
        copy.wait()
    sig = sig_ref[...]
    var_ref[...] = sig * sig
    tiles = off_ref.shape[1]
    slots = take_ref.shape[1]
    cells = pack_ref.shape[1]
    off = off_ref[...]
    frac = frac_ref[...]
    idx_ref[...] = jnp.concatenate([off, off + 1], axis=0).T
    w_ref[...] = jnp.concatenate([1.0 - frac, frac], axis=0).T
    keep[...] = jnp.broadcast_to(group_ref[...], (LANES, tiles)).T
    first = iota((tiles // 2, LANES), 1) < LANES // 2
    grp_ref[...] = jnp.where(
        first, keep[pl.ds(0, tiles // 2, 2), :], keep[pl.ds(1, tiles // 2, 2), :]
    )
    slot = slot_ref[...]
    wide = jnp.broadcast_to(slot, (LANES, tiles)).T
    for at in range(0, slots, LANES):
        take_ref[:, at : at + LANES] = one_hot(wide == iota((tiles, LANES), 1) + at)
    give_ref[...] = one_hot(jnp.broadcast_to(slot, (slots, tiles)) == iota((slots, tiles), 0))
    send = send_ref[...]
    wide = jnp.broadcast_to(send, (LANES, slots)).T
    for at in range(0, cells, LANES):
        pack_ref[:, at : at + LANES] = one_hot(wide == iota((slots, LANES), 1) + at)
    sum_ref[...] = one_hot(jnp.broadcast_to(send, (cells, slots)) == iota((cells, slots), 0))
    copies[-1].wait()


def sides(mats_ref, near, far):
    return apply_left(mats_ref[2], mats_ref[3], near) + apply_left(mats_ref[4], mats_ref[5], far)


def own_body(own_ref, mats_ref, part_ref):
    part_ref[...] = apply_left(mats_ref[0], mats_ref[1], own_ref[...])


def own_latent_body(own_ref, mats_ref, latent_ref, part_ref):
    part_ref[...] = latent_ref[...] + apply_left(mats_ref[0], mats_ref[1], own_ref[...])


def join_body(part_ref, near_ref, far_ref, mats_ref, out_ref, *sent_ref):
    out = part_ref[...] + sides(mats_ref, near_ref[...], far_ref[...])
    out_ref[...] = out
    for ref in sent_ref:
        ref[...] = out.astype(ref.dtype)


def density_body(part_ref, near_ref, far_ref, mats_ref, hz_ref, pack_ref, dens_ref, packed_ref):
    out = sides(mats_ref, near_ref[...], far_ref[...])
    dens = jnp.exp(part_ref[...] + apply_right(out, hz_ref[0], hz_ref[1]))
    dens_ref[...] = dens
    packed_ref[...] = mm(pack_ref[...], dens.astype(BF16)).astype(BF16)


def owner_body(sum_ref, back_ref, dens_ref, hz_ref, out_ref, sent_ref):
    grad = dens_ref[...] * mm(sum_ref[...], back_ref[...])
    out = apply_right(grad, hz_ref[0], hz_ref[1])
    out_ref[...] = out
    sent_ref[...] = out.astype(sent_ref.dtype)


def cone_body(
    got_ref, early_ref, late_ref, idx_ref, w_ref, grp_ref, take_ref, give_ref, obs_ref, var_ref,
    pred_ref, grad_ref, both, cells,
):
    early, samples, star_tile = early_ref.shape
    tiles = idx_ref.shape[0]
    depth = got_ref.shape[1]
    groups = obs_ref.shape[0]
    half = LANES // 2

    def rays(first, count):
        ref, first = (early_ref, first) if first < early else (late_ref, first - early)
        return ref[first : first + count].reshape(count * samples, star_tile)

    group_at = iota((groups, LANES), 0)
    lane_first = iota((AHEAD // 2, LANES), 1) < half
    got = got_ref[...]
    pred = jnp.zeros((groups, star_tile), F32)
    for base in range(0, tiles, AHEAD):
        span = pl.ds(base, AHEAD)
        idx = idx_ref[span, :]
        columns = mm(take_ref[span, :], got)
        for at in range(0, depth, LANES):
            piece = jnp.take_along_axis(
                columns[:, at : at + LANES], idx & (LANES - 1), axis=1
            )
            value = jnp.where(idx >= at, piece, value) if at else piece
        value = w_ref[span, :] * value
        both[span, :] = value + pltpu.roll(value, half, 1)
    for base in range(0, tiles, AHEAD):
        pair = jnp.where(
            lane_first, both[pl.ds(base, AHEAD // 2, 2), :], both[pl.ds(base + 1, AHEAD // 2, 2), :]
        )
        group = grp_ref[pl.ds(base // 2, AHEAD // 2), :]
        left = [
            jnp.where(group[i : i + 1] == group_at, pair[i : i + 1], 0.0)
            for i in range(AHEAD // 2)
        ]
        pred += mm(jnp.concatenate(left, axis=1).astype(BF16), rays(base, AHEAD))

    pred_ref[...] = pred
    resid = ((pred - obs_ref[...]) / var_ref[...]).astype(BF16)
    parts = depth // PART
    rows = 2 * parts
    at_row = iota((rows, LANES), 0)
    row_part = at_row & (parts - 1)
    row_second = (at_row & parts) != 0
    level = [(iota((16, LANES), 0) + at).astype(F32).astype(BF16) for at in range(0, PART, 16)]
    one = jnp.ones((16, LANES), BF16)
    zero = jnp.zeros((16, LANES), BF16)
    shift = PART.bit_length() - 1
    total = jnp.zeros(grad_ref.shape, F32)
    lane_first = iota((CHUNK // 2, LANES), 1) < half
    for base in range(0, tiles, CHUNK):
        back = mm_nt(resid, rays(base, CHUNK))
        group = grp_ref[pl.ds(base // 2, CHUNK // 2), :]
        picked = [
            jnp.sum(
                jnp.where(group[i : i + 1] == group_at, back[:, i * LANES : (i + 1) * LANES], 0.0),
                axis=0, keepdims=True,
            )
            for i in range(CHUNK // 2)
        ]
        picked = jnp.concatenate(picked, axis=0)
        swapped = pltpu.roll(picked, half, 1)
        even, odd = pl.ds(base, CHUNK // 2, 2), pl.ds(base + 1, CHUNK // 2, 2)
        weights = (
            jnp.where(lane_first, picked, swapped) * w_ref[even, :],
            jnp.where(lane_first, swapped, picked) * w_ref[odd, :],
        )
        spots = (idx_ref[even, :], idx_ref[odd, :])
        lanes = [(spot & (PART - 1)).astype(F32) for spot in spots]
        blocks = [lax.shift_right_logical(spot, shift) for spot in spots]
        blocks[1] = blocks[1] + parts
        for i in range(CHUNK // 2):
            left, right = [], []
            for which in (0, 1):
                kept = at_row == blocks[which][i : i + 1]
                left.append(jnp.where(kept, weights[which][i : i + 1], 0.0))
                lane = jnp.broadcast_to(lanes[which][i : i + 1], (16, LANES)).astype(BF16)
                right.append(
                    jnp.concatenate([jnp.where(lane == lv, one, zero) for lv in level], axis=0)
                )
            cells[(base // 2 + i) * rows : (base // 2 + i + 1) * rows, :] = mm_nt(
                jnp.concatenate(left, axis=1).astype(BF16), jnp.concatenate(right, axis=1)
            )
        if (base + CHUNK) % GIVE == 0:
            start = base + CHUNK - GIVE
            pieces = [cells[pl.ds(start * parts + at, GIVE, parts), :] for at in range(parts)]
            total += mm(
                give_ref[:, start : start + GIVE], jnp.concatenate(pieces, axis=1).astype(BF16)
            )
    grad_ref[...] = total.astype(BF16)


def cone_scratch(tiles, depth):
    return [pltpu.VMEM((tiles, LANES), F32), pltpu.VMEM((tiles * (depth // PART), PART), F32)]


def exchanged(values, axis):
    count = lax.axis_size(axis)
    return [
        lax.ppermute(
            values, axis,
            [pair for i in range(first, count - 1, 2) for pair in ((i, i + 1), (i + 1, i))],
        )
        for first in (0, 1)
    ]


def on_device(
    latent, observed, sigma, response, offsets, fractions, tile_group, tile_slot, send_index
):
    rows_x, rows_y, depth = latent.shape
    cells = rows_x * rows_y
    axes = ("cx", "cy")
    devices = lax.axis_size("cx") * lax.axis_size("cy")
    slots = devices * send_index.shape[2]
    tiles, samples, star_tile = response.shape
    groups = observed.shape[0] // star_tile
    own = latent.reshape(cells, depth)
    field_out = ((cells, depth), F32)
    sent_out = ((cells, depth), BF16)

    send = send_index.reshape(1, slots)
    ray_out = ((tiles // 2, samples, star_tile), BF16)
    near, far = exchanged(own.astype(BF16), "cx")
    hx, hy, hz, part, early = call(
        functools.partial(operators_body, rows_x, rows_y),
        [
            ((6, cells, cells), BF16), ((6, cells, cells), BF16), ((2, depth, depth), BF16),
            field_out, ray_out,
        ],
        hbm(own), hbm(response), hbm(send),
        scratch=[pltpu.VMEM((cells, depth), F32), pltpu.SemaphoreType.DMA((2,))],
        name="operators",
    )
    field, sent = call(join_body, [field_out, sent_out], part, near, far, hx, name="along_x")
    near, far = exchanged(sent, "cy")
    part, late, obs, var, idx, weight, grp, take, give, pack, add_up = call(
        tables_body,
        [
            field_out,
            ray_out,
            ((groups, star_tile), F32),
            ((groups, star_tile), F32),
            ((tiles, LANES), jnp.int32),
            ((tiles, LANES), F32),
            ((tiles // 2, LANES), jnp.int32),
            ((tiles, slots), BF16),
            ((slots, tiles), BF16),
            ((slots, cells), BF16),
            ((cells, slots), BF16),
        ],
        hbm(offsets), hbm(fractions), hbm(tile_group.reshape(1, tiles)),
        hbm(tile_slot.reshape(1, tiles)), hbm(send),
        hbm(observed.reshape(groups, star_tile)), hbm(sigma.reshape(groups, star_tile)),
        hbm(response), field, hy, hz,
        scratch=[
            pltpu.VMEM((samples, tiles), jnp.int32),
            pltpu.VMEM((samples, tiles), F32),
            pltpu.VMEM((1, tiles), jnp.int32),
            pltpu.VMEM((1, tiles), jnp.int32),
            pltpu.VMEM((1, slots), jnp.int32),
            pltpu.VMEM((groups, star_tile), F32),
            pltpu.VMEM((tiles, LANES), jnp.int32),
            pltpu.SemaphoreType.DMA((8,)),
        ],
        name="tables",
    )
    dens, packed = call(
        density_body, [field_out, ((slots, depth), BF16)],
        part, near, far, hy, hz, pack, name="density",
    )
    got = lax.all_to_all(packed, axes, split_axis=0, concat_axis=0, tiled=True)
    pred, grad = call(
        cone_body, [((groups, star_tile), F32), ((slots, depth), BF16)],
        got, early, late, idx, weight, grp, take, give, obs, var,
        scratch=cone_scratch(tiles, depth),
        limit=20,
        name="cones",
    )
    back = lax.all_to_all(grad, axes, split_axis=0, concat_axis=0, tiled=True)
    field, sent = call(owner_body, [field_out, sent_out], add_up, back, dens, hz, name="owners")
    near, far = exchanged(sent, "cy")
    (part,) = call(own_body, [field_out], field, hy, name="own_y")
    field, sent = call(join_body, [field_out, sent_out], part, near, far, hy, name="along_y")
    near, far = exchanged(sent, "cx")
    (part,) = call(own_latent_body, [field_out], field, hx, own, name="own_x")
    (gradient,) = call(join_body, [field_out], part, near, far, hx, name="finish")
    return gradient.reshape(rows_x, rows_y, depth), pred.reshape(-1)


def solution(mesh):
    both = ("cx", "cy")
    placed = (
        P("cx", "cy", None),
        P(both),
        P(both),
        P(both, None, None),
        P(None, both),
        P(None, both),
        P(both),
        P(both),
        P(both, None, None),
    )
    return jax.shard_map(
        on_device,
        mesh=mesh,
        in_specs=placed,
        out_specs=(P("cx", "cy", None), P(both)),
        check_vma=False,
    )
```

```python
import functools
import math

import jax
import jax.numpy as jnp
from jax import lax
from jax.experimental import pallas as pl
from jax.experimental.pallas import tpu as pltpu
from jax.sharding import PartitionSpec as P

REACH = 16
LANES = 128
F32 = jnp.float32
BF16 = jnp.bfloat16
AHEAD = 256
CHUNK = 256
GIVE = 256
FETCHES = 4
PART = 32


def tap_scale():
    total = 0.0
    for shift in range(-REACH, REACH + 1):
        a = math.sqrt(3.0) * abs(shift) / 8.0
        total += ((1.0 + a) * math.exp(-a)) ** 2
    return 0.8 / math.sqrt(total)


def split(values):
    high = values.astype(BF16)
    low = (values - high.astype(F32)).astype(BF16)
    return high, low


def mm(a, b):
    return jnp.dot(a, b, preferred_element_type=F32)


def mm_nt(a, b):
    return lax.dot_general(a, b, (((1,), (1,)), ((), ())), preferred_element_type=F32)


def iota(shape, dim):
    return lax.broadcasted_iota(jnp.int32, shape, dim)


def apply_left(mat_high, mat_low, values):
    if values.dtype == BF16:
        return mm(mat_high, values) + mm(mat_low, values)
    high, low = split(values)
    return mm(mat_high, high) + (mm(mat_high, low) + mm(mat_low, high))


def apply_right(values, mat_high, mat_low):
    high, low = split(values)
    return mm(high, mat_high) + (mm(low, mat_high) + mm(high, mat_low))


def hbm(array):
    return pltpu.with_memory_space_constraint(array, pltpu.HBM)


def is_hbm(array):
    return getattr(jax.typeof(array), "memory_space", None) is pltpu.HBM


def call(body, outs, *args, scratch=(), limit=16, name=None):
    shapes = [jax.ShapeDtypeStruct(s, d) for s, d in outs]
    moved = sum(math.prod(a.shape) * a.dtype.itemsize for a in args) + sum(
        math.prod(s.shape) * s.dtype.itemsize for s in shapes
    )
    return pl.pallas_call(
        body,
        out_shape=shapes,
        in_specs=[
            pl.BlockSpec(memory_space=pltpu.HBM if is_hbm(a) else pltpu.VMEM) for a in args
        ],
        out_specs=[pl.BlockSpec(memory_space=pltpu.VMEM)] * len(shapes),
        scratch_shapes=list(scratch),
        compiler_params=pltpu.CompilerParams(vmem_limit_bytes=limit << 20),
        cost_estimate=pl.CostEstimate(flops=0, bytes_accessed=moved, transcendentals=0),
        name=name,
    )(*args)


def taps_matrix(distance, kept):
    a = (math.sqrt(3.0) / 8.0) * jnp.abs(distance).astype(F32)
    value = (tap_scale() * (1.0 + a)) * jnp.exp(-a)
    return jnp.where(kept & (jnp.abs(distance) <= REACH), value, 0.0)


def operators(rows_x, rows_y, depth, hx_ref, hy_ref, hz_ref):
    cells = rows_x * rows_y
    out = iota((cells, cells), 0)
    inp = iota((cells, cells), 1)
    out_x, out_y = out // rows_y, out % rows_y
    inp_x, inp_y = inp // rows_y, inp % rows_y
    near_x = 2 * lax.rem(lax.axis_index("cx"), 2) - 1
    near_y = 2 * lax.rem(lax.axis_index("cy"), 2) - 1
    for at, side in enumerate((0, 1, -1)):
        high, low = split(taps_matrix(out_x - inp_x + side * near_x * rows_x, out_y == inp_y))
        hx_ref[2 * at], hx_ref[2 * at + 1] = high, low
        high, low = split(taps_matrix(out_y - inp_y + side * near_y * rows_y, out_x == inp_x))
        hy_ref[2 * at], hy_ref[2 * at + 1] = high, low
    shift = iota((depth, depth), 0) - iota((depth, depth), 1)
    high, low = split(taps_matrix(shift, shift == shift))
    hz_ref[0], hz_ref[1] = high, low


def one_hot(hits):
    return jnp.where(hits, 1.0, 0.0).astype(BF16)


def fetch(moves, sems):
    copies = [
        pltpu.make_async_copy(src, dst, sems.at[at]) for at, (src, dst) in enumerate(moves)
    ]
    for copy in copies:
        copy.start()
    return copies


def fetch_rays(resp_hbm, first, resp_ref, sems):
    chunk = resp_ref.shape[0] // FETCHES
    return fetch(
        [
            (resp_hbm.at[pl.ds(first + at, chunk)], resp_ref.at[pl.ds(at, chunk)])
            for at in range(0, resp_ref.shape[0], chunk)
        ],
        sems,
    )


def flip_rays(copies, resp_ref, flip_ref):
    tiles, samples, star_tile = resp_ref.shape
    chunk = tiles // FETCHES
    for copy, first in zip(copies, range(0, tiles, chunk)):
        copy.wait()
        rows = resp_ref[first : first + chunk].reshape(chunk * samples, star_tile)
        flip_ref[:, first * samples : (first + chunk) * samples] = rows.T


def operators_body(
    rows_x, rows_y, own_hbm, group_hbm, slot_hbm, resp_hbm,
    hx_ref, hy_ref, hz_ref, part_ref, resp_ref, flip_ref, grp_ref, take_ref, give_ref,
    own_ref, group_ref, slot_ref, keep, sems, ray_sems,
):
    copies = fetch([(own_hbm, own_ref), (group_hbm, group_ref), (slot_hbm, slot_ref)], sems)
    ray_copies = fetch_rays(resp_hbm, 0, resp_ref, ray_sems)
    operators(rows_x, rows_y, hz_ref.shape[1], hx_ref, hy_ref, hz_ref)
    for copy in copies:
        copy.wait()
    part_ref[...] = apply_left(hx_ref[0], hx_ref[1], own_ref[...])
    tiles, slots = take_ref.shape
    keep[...] = jnp.broadcast_to(group_ref[...], (LANES, tiles)).T
    lane_first = iota((tiles // 2, LANES), 1) < LANES // 2
    grp_ref[...] = jnp.where(
        lane_first, keep[pl.ds(0, tiles // 2, 2), :], keep[pl.ds(1, tiles // 2, 2), :]
    )
    slot = slot_ref[...]
    wide = jnp.broadcast_to(slot, (LANES, tiles)).T
    for at in range(0, slots, LANES):
        take_ref[:, at : at + LANES] = one_hot(wide == iota((tiles, LANES), 1) + at)
    give_ref[...] = one_hot(jnp.broadcast_to(slot, (slots, tiles)) == iota((slots, tiles), 0))
    flip_rays(ray_copies, resp_ref, flip_ref)


def tables_body(
    off_hbm, frac_hbm, send_hbm, obs_hbm, sig_hbm, resp_hbm,
    field_ref, hy_ref, hz_ref,
    part_ref, resp_ref, flip_ref, obs_ref, var_ref,
    idx_ref, w_ref, pack_ref, sum_ref,
    off_ref, frac_ref, send_ref, sig_ref, sems, ray_sems,
):
    copies = fetch(
        [
            (off_hbm, off_ref), (frac_hbm, frac_ref), (send_hbm, send_ref),
            (obs_hbm, obs_ref), (sig_hbm, sig_ref),
        ],
        sems,
    )
    first = resp_hbm.shape[0] - resp_ref.shape[0]
    ray_copies = fetch_rays(resp_hbm, first, resp_ref, ray_sems)
    part = apply_left(hy_ref[0], hy_ref[1], field_ref[...])
    part_ref[...] = apply_right(part, hz_ref[0], hz_ref[1])
    for copy in copies:
        copy.wait()
    sig = sig_ref[...]
    var_ref[...] = sig * sig
    slots, cells = pack_ref.shape
    off = off_ref[...]
    frac = frac_ref[...]
    idx_ref[...] = jnp.concatenate([off, off + 1], axis=0).T
    w_ref[...] = jnp.concatenate([1.0 - frac, frac], axis=0).T
    capacity, devices = send_ref.shape
    wide = jnp.concatenate(
        [
            jnp.broadcast_to(send_ref[:, at : at + 1], (capacity, LANES))
            for at in range(devices)
        ],
        axis=0,
    )
    for at in range(0, cells, LANES):
        pack_ref[:, at : at + LANES] = one_hot(wide == iota((slots, LANES), 1) + at)
    send = wide.T[0:1]
    sum_ref[...] = one_hot(jnp.broadcast_to(send, (cells, slots)) == iota((cells, slots), 0))
    flip_rays(ray_copies, resp_ref, flip_ref)


def sides(mats_ref, near, far):
    return apply_left(mats_ref[2], mats_ref[3], near) + apply_left(mats_ref[4], mats_ref[5], far)


def own_body(own_ref, mats_ref, part_ref):
    part_ref[...] = apply_left(mats_ref[0], mats_ref[1], own_ref[...])


def own_latent_body(own_ref, mats_ref, latent_ref, part_ref):
    part_ref[...] = latent_ref[...] + apply_left(mats_ref[0], mats_ref[1], own_ref[...])


def join_body(part_ref, near_ref, far_ref, mats_ref, out_ref, *sent_ref):
    out = part_ref[...] + sides(mats_ref, near_ref[...], far_ref[...])
    out_ref[...] = out
    for ref in sent_ref:
        ref[...] = out.astype(ref.dtype)


def density_body(part_ref, near_ref, far_ref, mats_ref, hz_ref, pack_ref, dens_ref, packed_ref):
    out = sides(mats_ref, near_ref[...], far_ref[...])
    dens = jnp.exp(part_ref[...] + apply_right(out, hz_ref[0], hz_ref[1]))
    dens_ref[...] = dens
    packed_ref[...] = mm(pack_ref[...], dens.astype(BF16)).astype(BF16)


def owner_body(sum_ref, back_ref, dens_ref, hz_ref, out_ref, sent_ref):
    grad = dens_ref[...] * mm(sum_ref[...], back_ref[...])
    out = apply_right(grad, hz_ref[0], hz_ref[1])
    out_ref[...] = out
    sent_ref[...] = out.astype(sent_ref.dtype)


def cone_body(
    got_ref, early_ref, late_ref, flip_early_ref, flip_late_ref, idx_ref, w_ref, grp_ref, take_ref, give_ref, obs_ref, var_ref,
    pred_ref, grad_ref, both, cells,
):
    early, samples, star_tile = early_ref.shape
    tiles = idx_ref.shape[0]
    depth = got_ref.shape[1]
    groups = obs_ref.shape[0]
    half = LANES // 2

    def rays(first, count):
        ref, first = (early_ref, first) if first < early else (late_ref, first - early)
        return ref[first : first + count].reshape(count * samples, star_tile)

    def flipped(first, count):
        ref, first = (flip_early_ref, first) if first < early else (flip_late_ref, first - early)
        return ref[:, first * samples : (first + count) * samples]

    group_at = iota((groups, LANES), 0)
    lane_first = iota((AHEAD // 2, LANES), 1) < half
    got = got_ref[...]
    pred = jnp.zeros((groups, star_tile), F32)
    for base in range(0, tiles, AHEAD):
        span = pl.ds(base, AHEAD)
        idx = idx_ref[span, :]
        columns = mm(take_ref[span, :], got)
        for at in range(0, depth, LANES):
            piece = jnp.take_along_axis(
                columns[:, at : at + LANES], idx & (LANES - 1), axis=1
            )
            value = jnp.where(idx >= at, piece, value) if at else piece
        value = w_ref[span, :] * value
        both[span, :] = value + pltpu.roll(value, half, 1)
    for base in range(0, tiles, AHEAD):
        pair = jnp.where(
            lane_first, both[pl.ds(base, AHEAD // 2, 2), :], both[pl.ds(base + 1, AHEAD // 2, 2), :]
        )
        group = grp_ref[pl.ds(base // 2, AHEAD // 2), :]
        left = [
            jnp.where(group[i : i + 1] == group_at, pair[i : i + 1], 0.0)
            for i in range(AHEAD // 2)
        ]
        pred += mm(jnp.concatenate(left, axis=1).astype(BF16), rays(base, AHEAD))

    pred_ref[...] = pred
    resid = ((pred - obs_ref[...]) / var_ref[...]).astype(BF16)
    parts = depth // PART
    rows = 2 * parts
    at_row = iota((rows, LANES), 0)
    row_part = at_row & (parts - 1)
    row_second = (at_row & parts) != 0
    level = [(iota((16, LANES), 0) + at).astype(F32).astype(BF16) for at in range(0, PART, 16)]
    one = jnp.ones((16, LANES), BF16)
    zero = jnp.zeros((16, LANES), BF16)
    shift = PART.bit_length() - 1
    total = jnp.zeros(grad_ref.shape, F32)
    lane_first = iota((CHUNK // 2, LANES), 1) < half
    for base in range(0, tiles, CHUNK):
        back = mm(resid, flipped(base, CHUNK))
        group = grp_ref[pl.ds(base // 2, CHUNK // 2), :]
        picked = [
            jnp.sum(
                jnp.where(group[i : i + 1] == group_at, back[:, i * LANES : (i + 1) * LANES], 0.0),
                axis=0, keepdims=True,
            )
            for i in range(CHUNK // 2)
        ]
        picked = jnp.concatenate(picked, axis=0)
        swapped = pltpu.roll(picked, half, 1)
        even, odd = pl.ds(base, CHUNK // 2, 2), pl.ds(base + 1, CHUNK // 2, 2)
        weights = (
            jnp.where(lane_first, picked, swapped) * w_ref[even, :],
            jnp.where(lane_first, swapped, picked) * w_ref[odd, :],
        )
        spots = (idx_ref[even, :], idx_ref[odd, :])
        lanes = [(spot & (PART - 1)).astype(F32) for spot in spots]
        blocks = [lax.shift_right_logical(spot, shift) for spot in spots]
        blocks[1] = blocks[1] + parts
        for i in range(CHUNK // 2):
            left, right = [], []
            for which in (0, 1):
                kept = at_row == blocks[which][i : i + 1]
                left.append(jnp.where(kept, weights[which][i : i + 1], 0.0))
                lane = jnp.broadcast_to(lanes[which][i : i + 1], (16, LANES)).astype(BF16)
                right.append(
                    jnp.concatenate([jnp.where(lane == lv, one, zero) for lv in level], axis=0)
                )
            cells[(base // 2 + i) * rows : (base // 2 + i + 1) * rows, :] = mm_nt(
                jnp.concatenate(left, axis=1).astype(BF16), jnp.concatenate(right, axis=1)
            )
        if (base + CHUNK) % GIVE == 0:
            start = base + CHUNK - GIVE
            pieces = [cells[pl.ds(start * parts + at, GIVE, parts), :] for at in range(parts)]
            total += mm(
                give_ref[:, start : start + GIVE], jnp.concatenate(pieces, axis=1).astype(BF16)
            )
    grad_ref[...] = total.astype(BF16)


def cone_scratch(tiles, depth):
    return [pltpu.VMEM((tiles, LANES), F32), pltpu.VMEM((tiles * (depth // PART), PART), F32)]


def exchanged(values, axis):
    count = lax.axis_size(axis)
    return [
        lax.ppermute(
            values, axis,
            [pair for i in range(first, count - 1, 2) for pair in ((i, i + 1), (i + 1, i))],
        )
        for first in (0, 1)
    ]


def on_device(
    latent, observed, sigma, response, offsets, fractions, tile_group, tile_slot, send_index
):
    rows_x, rows_y, depth = latent.shape
    cells = rows_x * rows_y
    axes = ("cx", "cy")
    devices = lax.axis_size("cx") * lax.axis_size("cy")
    slots = devices * send_index.shape[2]
    tiles, samples, star_tile = response.shape
    groups = observed.shape[0] // star_tile
    own = latent.reshape(cells, depth)
    field_out = ((cells, depth), F32)
    sent_out = ((cells, depth), BF16)

    send = send_index.reshape(devices, -1).T
    flip_out = ((star_tile, tiles // 2 * samples), BF16)
    ray_out = ((tiles // 2, samples, star_tile), BF16)
    near, far = exchanged(own.astype(BF16), "cx")
    hx, hy, hz, part, early, flip_early, grp, take, give = call(
        functools.partial(operators_body, rows_x, rows_y),
        [
            ((6, cells, cells), BF16), ((6, cells, cells), BF16), ((2, depth, depth), BF16),
            field_out, ray_out, flip_out,
            ((tiles // 2, LANES), jnp.int32), ((tiles, slots), BF16), ((slots, tiles), BF16),
        ],
        hbm(own), hbm(tile_group.reshape(1, tiles)), hbm(tile_slot.reshape(1, tiles)),
        hbm(response),
        scratch=[
            pltpu.VMEM((cells, depth), F32),
            pltpu.VMEM((1, tiles), jnp.int32),
            pltpu.VMEM((1, tiles), jnp.int32),
            pltpu.VMEM((tiles, LANES), jnp.int32),
            pltpu.SemaphoreType.DMA((3,)),
            pltpu.SemaphoreType.DMA((FETCHES,)),
        ],
        name="operators",
    )
    field, sent = call(join_body, [field_out, sent_out], part, near, far, hx, name="along_x")
    near, far = exchanged(sent, "cy")
    part, late, flip_late, obs, var, idx, weight, pack, add_up = call(
        tables_body,
        [
            field_out,
            ray_out,
            flip_out,
            ((groups, star_tile), F32),
            ((groups, star_tile), F32),
            ((tiles, LANES), jnp.int32),
            ((tiles, LANES), F32),
            ((slots, cells), BF16),
            ((cells, slots), BF16),
        ],
        hbm(offsets), hbm(fractions), hbm(send),
        hbm(observed.reshape(groups, star_tile)), hbm(sigma.reshape(groups, star_tile)),
        hbm(response), field, hy, hz,
        scratch=[
            pltpu.VMEM((samples, tiles), jnp.int32),
            pltpu.VMEM((samples, tiles), F32),
            pltpu.VMEM(send.shape, jnp.int32),
            pltpu.VMEM((groups, star_tile), F32),
            pltpu.SemaphoreType.DMA((5,)),
            pltpu.SemaphoreType.DMA((FETCHES,)),
        ],
        name="tables",
    )
    dens, packed = call(
        density_body, [field_out, ((slots, depth), BF16)],
        part, near, far, hy, hz, pack, name="density",
    )
    got = lax.all_to_all(packed, axes, split_axis=0, concat_axis=0, tiled=True)
    pred, grad = call(
        cone_body, [((groups, star_tile), F32), ((slots, depth), BF16)],
        got, early, late, flip_early, flip_late, idx, weight, grp, take, give, obs, var,
        scratch=cone_scratch(tiles, depth),
        limit=20,
        name="cones",
    )
    back = lax.all_to_all(grad, axes, split_axis=0, concat_axis=0, tiled=True)
    field, sent = call(owner_body, [field_out, sent_out], add_up, back, dens, hz, name="owners")
    near, far = exchanged(sent, "cy")
    (part,) = call(own_body, [field_out], field, hy, name="own_y")
    field, sent = call(join_body, [field_out, sent_out], part, near, far, hy, name="along_y")
    near, far = exchanged(sent, "cx")
    (part,) = call(own_latent_body, [field_out], field, hx, own, name="own_x")
    (gradient,) = call(join_body, [field_out], part, near, far, hx, name="finish")
    return gradient.reshape(rows_x, rows_y, depth), pred.reshape(-1)


def solution(mesh):
    both = ("cx", "cy")
    placed = (
        P("cx", "cy", None),
        P(both),
        P(both),
        P(both, None, None),
        P(None, both),
        P(None, both),
        P(both),
        P(both),
        P(both, None, None),
    )
    return jax.shard_map(
        on_device,
        mesh=mesh,
        in_specs=placed,
        out_specs=(P("cx", "cy", None), P(both)),
        check_vma=False,
    )
```

```python
import functools
import math

import jax
import jax.numpy as jnp
from jax import lax
from jax.experimental import pallas as pl
from jax.experimental.pallas import tpu as pltpu
from jax.sharding import PartitionSpec as P

REACH = 16
LANES = 128
F32 = jnp.float32
BF16 = jnp.bfloat16
AHEAD = 256
CHUNK = 256
GIVE = 256
FETCHES = 4
PART = 32


def tap_scale():
    total = 0.0
    for shift in range(-REACH, REACH + 1):
        a = math.sqrt(3.0) * abs(shift) / 8.0
        total += ((1.0 + a) * math.exp(-a)) ** 2
    return 0.8 / math.sqrt(total)


def split(values):
    high = values.astype(BF16)
    low = (values - high.astype(F32)).astype(BF16)
    return high, low


def mm(a, b):
    return jnp.dot(a, b, preferred_element_type=F32)


def mm_nt(a, b):
    return lax.dot_general(a, b, (((1,), (1,)), ((), ())), preferred_element_type=F32)


def iota(shape, dim):
    return lax.broadcasted_iota(jnp.int32, shape, dim)


def apply_left(mat_high, mat_low, values):
    if values.dtype == BF16:
        return mm(mat_high, values)
    high, low = split(values)
    return mm(mat_high, high) + (mm(mat_high, low) + mm(mat_low, high))


def apply_right(values, mat_high, mat_low):
    high, low = split(values)
    return mm(high, mat_high) + (mm(low, mat_high) + mm(high, mat_low))


def hbm(array):
    return pltpu.with_memory_space_constraint(array, pltpu.HBM)


def is_hbm(array):
    return getattr(jax.typeof(array), "memory_space", None) is pltpu.HBM


def call(body, outs, *args, scratch=(), limit=16, name=None):
    shapes = [jax.ShapeDtypeStruct(s, d) for s, d in outs]
    moved = sum(math.prod(a.shape) * a.dtype.itemsize for a in args) + sum(
        math.prod(s.shape) * s.dtype.itemsize for s in shapes
    )
    return pl.pallas_call(
        body,
        out_shape=shapes,
        in_specs=[
            pl.BlockSpec(memory_space=pltpu.HBM if is_hbm(a) else pltpu.VMEM) for a in args
        ],
        out_specs=[pl.BlockSpec(memory_space=pltpu.VMEM)] * len(shapes),
        scratch_shapes=list(scratch),
        compiler_params=pltpu.CompilerParams(vmem_limit_bytes=limit << 20),
        cost_estimate=pl.CostEstimate(flops=0, bytes_accessed=moved, transcendentals=0),
        name=name,
    )(*args)


def taps_matrix(distance, kept):
    a = (math.sqrt(3.0) / 8.0) * jnp.abs(distance).astype(F32)
    value = (tap_scale() * (1.0 + a)) * jnp.exp(-a)
    return jnp.where(kept & (jnp.abs(distance) <= REACH), value, 0.0)


def operators(rows_x, rows_y, depth, hx_ref, hy_ref, hz_ref):
    cells = rows_x * rows_y
    out = iota((cells, cells), 0)
    inp = iota((cells, cells), 1)
    out_x, out_y = out // rows_y, out % rows_y
    inp_x, inp_y = inp // rows_y, inp % rows_y
    near_x = 2 * lax.rem(lax.axis_index("cx"), 2) - 1
    near_y = 2 * lax.rem(lax.axis_index("cy"), 2) - 1
    for at, side in enumerate((0, 1, -1)):
        high, low = split(taps_matrix(out_x - inp_x + side * near_x * rows_x, out_y == inp_y))
        hx_ref[2 * at], hx_ref[2 * at + 1] = high, low
        high, low = split(taps_matrix(out_y - inp_y + side * near_y * rows_y, out_x == inp_x))
        hy_ref[2 * at], hy_ref[2 * at + 1] = high, low
    shift = iota((depth, depth), 0) - iota((depth, depth), 1)
    high, low = split(taps_matrix(shift, shift == shift))
    hz_ref[0], hz_ref[1] = high, low


def one_hot(hits):
    return jnp.where(hits, 1.0, 0.0).astype(BF16)


def fetch(moves, sems):
    copies = [
        pltpu.make_async_copy(src, dst, sems.at[at]) for at, (src, dst) in enumerate(moves)
    ]
    for copy in copies:
        copy.start()
    return copies


def fetch_rays(resp_hbm, first, resp_ref, sems):
    chunk = resp_ref.shape[0] // FETCHES
    return fetch(
        [
            (resp_hbm.at[pl.ds(first + at, chunk)], resp_ref.at[pl.ds(at, chunk)])
            for at in range(0, resp_ref.shape[0], chunk)
        ],
        sems,
    )


def flip_rays(copies, resp_ref, flip_ref):
    tiles, samples, star_tile = resp_ref.shape
    chunk = tiles // FETCHES
    for copy, first in zip(copies, range(0, tiles, chunk)):
        copy.wait()
        rows = resp_ref[first : first + chunk].reshape(chunk * samples, star_tile)
        flip_ref[:, first * samples : (first + chunk) * samples] = rows.T


def operators_body(
    rows_x, rows_y, own_hbm, group_hbm, slot_hbm, resp_hbm,
    hx_ref, hy_ref, hz_ref, part_ref, resp_ref, flip_ref, grp_ref, take_ref, give_ref,
    own_ref, group_ref, slot_ref, keep, sems, ray_sems,
):
    copies = fetch([(own_hbm, own_ref), (group_hbm, group_ref), (slot_hbm, slot_ref)], sems)
    ray_copies = fetch_rays(resp_hbm, 0, resp_ref, ray_sems)
    operators(rows_x, rows_y, hz_ref.shape[1], hx_ref, hy_ref, hz_ref)
    for copy in copies:
        copy.wait()
    part_ref[...] = apply_left(hx_ref[0], hx_ref[1], own_ref[...])
    tiles, slots = take_ref.shape
    keep[...] = jnp.broadcast_to(group_ref[...], (LANES, tiles)).T
    lane_first = iota((tiles // 2, LANES), 1) < LANES // 2
    grp_ref[...] = jnp.where(
        lane_first, keep[pl.ds(0, tiles // 2, 2), :], keep[pl.ds(1, tiles // 2, 2), :]
    )
    slot = slot_ref[...]
    wide = jnp.broadcast_to(slot, (LANES, tiles)).T
    for at in range(0, slots, LANES):
        take_ref[:, at : at + LANES] = one_hot(wide == iota((tiles, LANES), 1) + at)
    give_ref[...] = one_hot(jnp.broadcast_to(slot, (slots, tiles)) == iota((slots, tiles), 0))
    flip_rays(ray_copies, resp_ref, flip_ref)


def tables_body(
    off_hbm, frac_hbm, send_hbm, obs_hbm, sig_hbm, resp_hbm,
    field_ref, hy_ref, hz_ref,
    part_ref, resp_ref, flip_ref, obs_ref, var_ref,
    idx_ref, w_ref, pack_ref, sum_ref,
    off_ref, frac_ref, send_ref, sig_ref, sems, ray_sems,
):
    copies = fetch(
        [
            (off_hbm, off_ref), (frac_hbm, frac_ref), (send_hbm, send_ref),
            (obs_hbm, obs_ref), (sig_hbm, sig_ref),
        ],
        sems,
    )
    first = resp_hbm.shape[0] - resp_ref.shape[0]
    ray_copies = fetch_rays(resp_hbm, first, resp_ref, ray_sems)
    part = apply_left(hy_ref[0], hy_ref[1], field_ref[...])
    part_ref[...] = apply_right(part, hz_ref[0], hz_ref[1])
    for copy in copies:
        copy.wait()
    sig = sig_ref[...]
    var_ref[...] = sig * sig
    slots, cells = pack_ref.shape
    off = off_ref[...]
    frac = frac_ref[...]
    idx_ref[...] = jnp.concatenate([off, off + 1], axis=0).T
    w_ref[...] = jnp.concatenate([1.0 - frac, frac], axis=0).T
    capacity, devices = send_ref.shape
    wide = jnp.concatenate(
        [
            jnp.broadcast_to(send_ref[:, at : at + 1], (capacity, LANES))
            for at in range(devices)
        ],
        axis=0,
    )
    for at in range(0, cells, LANES):
        pack_ref[:, at : at + LANES] = one_hot(wide == iota((slots, LANES), 1) + at)
    send = wide.T[0:1]
    sum_ref[...] = one_hot(jnp.broadcast_to(send, (cells, slots)) == iota((cells, slots), 0))
    flip_rays(ray_copies, resp_ref, flip_ref)


def sides(mats_ref, near, far):
    return apply_left(mats_ref[2], mats_ref[3], near) + apply_left(mats_ref[4], mats_ref[5], far)


def own_body(own_ref, mats_ref, part_ref):
    part_ref[...] = apply_left(mats_ref[0], mats_ref[1], own_ref[...])


def own_latent_body(own_ref, mats_ref, latent_ref, part_ref):
    part_ref[...] = latent_ref[...] + apply_left(mats_ref[0], mats_ref[1], own_ref[...])


def join_body(part_ref, near_ref, far_ref, mats_ref, out_ref, *sent_ref):
    out = part_ref[...] + sides(mats_ref, near_ref[...], far_ref[...])
    out_ref[...] = out
    for ref in sent_ref:
        ref[...] = out.astype(ref.dtype)


def density_body(part_ref, near_ref, far_ref, mats_ref, hz_ref, pack_ref, dens_ref, packed_ref):
    out = sides(mats_ref, near_ref[...], far_ref[...])
    dens = jnp.exp(part_ref[...] + apply_right(out, hz_ref[0], hz_ref[1]))
    dens_ref[...] = dens
    packed_ref[...] = mm(pack_ref[...], dens.astype(BF16)).astype(BF16)


def owner_body(sum_ref, back_ref, dens_ref, hz_ref, out_ref, sent_ref):
    grad = dens_ref[...] * mm(sum_ref[...], back_ref[...])
    out = mm(grad.astype(BF16), hz_ref[0])
    out_ref[...] = out
    sent_ref[...] = out.astype(sent_ref.dtype)


def cone_body(
    got_ref, early_ref, late_ref, flip_early_ref, flip_late_ref, idx_ref, w_ref, grp_ref, take_ref, give_ref, obs_ref, var_ref,
    pred_ref, grad_ref, both, cells,
):
    early, samples, star_tile = early_ref.shape
    tiles = idx_ref.shape[0]
    depth = got_ref.shape[1]
    groups = obs_ref.shape[0]
    half = LANES // 2

    def rays(first, count):
        ref, first = (early_ref, first) if first < early else (late_ref, first - early)
        return ref[first : first + count].reshape(count * samples, star_tile)

    def flipped(first, count):
        ref, first = (flip_early_ref, first) if first < early else (flip_late_ref, first - early)
        return ref[:, first * samples : (first + count) * samples]

    group_at = iota((groups, LANES), 0)
    lane_first = iota((AHEAD // 2, LANES), 1) < half
    got = got_ref[...]
    pred = jnp.zeros((groups, star_tile), F32)
    for base in range(0, tiles, AHEAD):
        span = pl.ds(base, AHEAD)
        idx = idx_ref[span, :]
        columns = mm(take_ref[span, :], got)
        for at in range(0, depth, LANES):
            piece = jnp.take_along_axis(
                columns[:, at : at + LANES], idx & (LANES - 1), axis=1
            )
            value = jnp.where(idx >= at, piece, value) if at else piece
        value = w_ref[span, :] * value
        both[span, :] = value + pltpu.roll(value, half, 1)
    for base in range(0, tiles, AHEAD):
        pair = jnp.where(
            lane_first, both[pl.ds(base, AHEAD // 2, 2), :], both[pl.ds(base + 1, AHEAD // 2, 2), :]
        )
        group = grp_ref[pl.ds(base // 2, AHEAD // 2), :]
        left = [
            jnp.where(group[i : i + 1] == group_at, pair[i : i + 1], 0.0)
            for i in range(AHEAD // 2)
        ]
        pred += mm(jnp.concatenate(left, axis=1).astype(BF16), rays(base, AHEAD))

    pred_ref[...] = pred
    resid = ((pred - obs_ref[...]) / var_ref[...]).astype(BF16)
    parts = depth // PART
    rows = 2 * parts
    at_row = iota((rows, LANES), 0)
    row_part = at_row & (parts - 1)
    row_second = (at_row & parts) != 0
    level = [(iota((16, LANES), 0) + at).astype(F32).astype(BF16) for at in range(0, PART, 16)]
    one = jnp.ones((16, LANES), BF16)
    zero = jnp.zeros((16, LANES), BF16)
    shift = PART.bit_length() - 1
    total = jnp.zeros(grad_ref.shape, F32)
    lane_first = iota((CHUNK // 2, LANES), 1) < half
    for base in range(0, tiles, CHUNK):
        back = mm(resid, flipped(base, CHUNK))
        group = grp_ref[pl.ds(base // 2, CHUNK // 2), :]
        picked = [
            jnp.sum(
                jnp.where(group[i : i + 1] == group_at, back[:, i * LANES : (i + 1) * LANES], 0.0),
                axis=0, keepdims=True,
            )
            for i in range(CHUNK // 2)
        ]
        picked = jnp.concatenate(picked, axis=0)
        swapped = pltpu.roll(picked, half, 1)
        even, odd = pl.ds(base, CHUNK // 2, 2), pl.ds(base + 1, CHUNK // 2, 2)
        weights = (
            jnp.where(lane_first, picked, swapped) * w_ref[even, :],
            jnp.where(lane_first, swapped, picked) * w_ref[odd, :],
        )
        spots = (idx_ref[even, :], idx_ref[odd, :])
        lanes = [(spot & (PART - 1)).astype(F32) for spot in spots]
        blocks = [lax.shift_right_logical(spot, shift) for spot in spots]
        blocks[1] = blocks[1] + parts
        for i in range(CHUNK // 2):
            left, right = [], []
            for which in (0, 1):
                kept = at_row == blocks[which][i : i + 1]
                left.append(jnp.where(kept, weights[which][i : i + 1], 0.0))
                lane = jnp.broadcast_to(lanes[which][i : i + 1], (16, LANES)).astype(BF16)
                right.append(
                    jnp.concatenate([jnp.where(lane == lv, one, zero) for lv in level], axis=0)
                )
            cells[(base // 2 + i) * rows : (base // 2 + i + 1) * rows, :] = mm_nt(
                jnp.concatenate(left, axis=1).astype(BF16), jnp.concatenate(right, axis=1)
            )
        if (base + CHUNK) % GIVE == 0:
            start = base + CHUNK - GIVE
            pieces = [cells[pl.ds(start * parts + at, GIVE, parts), :] for at in range(parts)]
            total += mm(
                give_ref[:, start : start + GIVE], jnp.concatenate(pieces, axis=1).astype(BF16)
            )
    grad_ref[...] = total.astype(BF16)


def cone_scratch(tiles, depth):
    return [pltpu.VMEM((tiles, LANES), F32), pltpu.VMEM((tiles * (depth // PART), PART), F32)]


def exchanged(values, axis):
    count = lax.axis_size(axis)
    return [
        lax.ppermute(
            values, axis,
            [pair for i in range(first, count - 1, 2) for pair in ((i, i + 1), (i + 1, i))],
        )
        for first in (0, 1)
    ]


def on_device(
    latent, observed, sigma, response, offsets, fractions, tile_group, tile_slot, send_index
):
    rows_x, rows_y, depth = latent.shape
    cells = rows_x * rows_y
    axes = ("cx", "cy")
    devices = lax.axis_size("cx") * lax.axis_size("cy")
    slots = devices * send_index.shape[2]
    tiles, samples, star_tile = response.shape
    groups = observed.shape[0] // star_tile
    own = latent.reshape(cells, depth)
    field_out = ((cells, depth), F32)
    sent_out = ((cells, depth), BF16)

    send = send_index.reshape(devices, -1).T
    flip_out = ((star_tile, tiles // 2 * samples), BF16)
    ray_out = ((tiles // 2, samples, star_tile), BF16)
    near, far = exchanged(own.astype(BF16), "cx")
    hx, hy, hz, part, early, flip_early, grp, take, give = call(
        functools.partial(operators_body, rows_x, rows_y),
        [
            ((6, cells, cells), BF16), ((6, cells, cells), BF16), ((2, depth, depth), BF16),
            field_out, ray_out, flip_out,
            ((tiles // 2, LANES), jnp.int32), ((tiles, slots), BF16), ((slots, tiles), BF16),
        ],
        hbm(own), hbm(tile_group.reshape(1, tiles)), hbm(tile_slot.reshape(1, tiles)),
        hbm(response),
        scratch=[
            pltpu.VMEM((cells, depth), F32),
            pltpu.VMEM((1, tiles), jnp.int32),
            pltpu.VMEM((1, tiles), jnp.int32),
            pltpu.VMEM((tiles, LANES), jnp.int32),
            pltpu.SemaphoreType.DMA((3,)),
            pltpu.SemaphoreType.DMA((FETCHES,)),
        ],
        name="operators",
    )
    field, sent = call(join_body, [field_out, sent_out], part, near, far, hx, name="along_x")
    near, far = exchanged(sent, "cy")
    part, late, flip_late, obs, var, idx, weight, pack, add_up = call(
        tables_body,
        [
            field_out,
            ray_out,
            flip_out,
            ((groups, star_tile), F32),
            ((groups, star_tile), F32),
            ((tiles, LANES), jnp.int32),
            ((tiles, LANES), F32),
            ((slots, cells), BF16),
            ((cells, slots), BF16),
        ],
        hbm(offsets), hbm(fractions), hbm(send),
        hbm(observed.reshape(groups, star_tile)), hbm(sigma.reshape(groups, star_tile)),
        hbm(response), field, hy, hz,
        scratch=[
            pltpu.VMEM((samples, tiles), jnp.int32),
            pltpu.VMEM((samples, tiles), F32),
            pltpu.VMEM(send.shape, jnp.int32),
            pltpu.VMEM((groups, star_tile), F32),
            pltpu.SemaphoreType.DMA((5,)),
            pltpu.SemaphoreType.DMA((FETCHES,)),
        ],
        name="tables",
    )
    dens, packed = call(
        density_body, [field_out, ((slots, depth), BF16)],
        part, near, far, hy, hz, pack, name="density",
    )
    got = lax.all_to_all(packed, axes, split_axis=0, concat_axis=0, tiled=True)
    pred, grad = call(
        cone_body, [((groups, star_tile), F32), ((slots, depth), BF16)],
        got, early, late, flip_early, flip_late, idx, weight, grp, take, give, obs, var,
        scratch=cone_scratch(tiles, depth),
        limit=20,
        name="cones",
    )
    back = lax.all_to_all(grad, axes, split_axis=0, concat_axis=0, tiled=True)
    field, sent = call(owner_body, [field_out, sent_out], add_up, back, dens, hz, name="owners")
    near, far = exchanged(sent, "cy")
    (part,) = call(own_body, [field_out], field, hy, name="own_y")
    field, sent = call(join_body, [field_out, sent_out], part, near, far, hy, name="along_y")
    near, far = exchanged(sent, "cx")
    (part,) = call(own_latent_body, [field_out], field, hx, own, name="own_x")
    (gradient,) = call(join_body, [field_out], part, near, far, hx, name="finish")
    return gradient.reshape(rows_x, rows_y, depth), pred.reshape(-1)


def solution(mesh):
    both = ("cx", "cy")
    placed = (
        P("cx", "cy", None),
        P(both),
        P(both),
        P(both, None, None),
        P(None, both),
        P(None, both),
        P(both),
        P(both),
        P(both, None, None),
    )
    return jax.shard_map(
        on_device,
        mesh=mesh,
        in_specs=placed,
        out_specs=(P("cx", "cy", None), P(both)),
        check_vma=False,
    )
```

```python
import functools
import math

import jax
import jax.numpy as jnp
from jax import lax
from jax.experimental import pallas as pl
from jax.experimental.pallas import tpu as pltpu
from jax.sharding import PartitionSpec as P

REACH = 16
LANES = 128
F32 = jnp.float32
BF16 = jnp.bfloat16
AHEAD = 256
CHUNK = 256
GIVE = 256
FETCHES = 8
PART = 32


def tap_scale():
    total = 0.0
    for shift in range(-REACH, REACH + 1):
        a = math.sqrt(3.0) * abs(shift) / 8.0
        total += ((1.0 + a) * math.exp(-a)) ** 2
    return 0.8 / math.sqrt(total)


def split(values):
    high = values.astype(BF16)
    low = (values - high.astype(F32)).astype(BF16)
    return high, low


def mm(a, b):
    return jnp.dot(a, b, preferred_element_type=F32)


def mm_nt(a, b):
    return lax.dot_general(a, b, (((1,), (1,)), ((), ())), preferred_element_type=F32)


def iota(shape, dim):
    return lax.broadcasted_iota(jnp.int32, shape, dim)


def apply_left(mat_high, mat_low, values):
    if values.dtype == BF16:
        return mm(mat_high, values)
    high, low = split(values)
    return mm(mat_high, high) + (mm(mat_high, low) + mm(mat_low, high))


def apply_right(values, mat_high, mat_low):
    high, low = split(values)
    return mm(high, mat_high) + (mm(low, mat_high) + mm(high, mat_low))


def hbm(array):
    return pltpu.with_memory_space_constraint(array, pltpu.HBM)


def is_hbm(array):
    return getattr(jax.typeof(array), "memory_space", None) is pltpu.HBM


def call(body, outs, *args, scratch=(), limit=16, name=None):
    shapes = [jax.ShapeDtypeStruct(s, d) for s, d in outs]
    moved = sum(math.prod(a.shape) * a.dtype.itemsize for a in args) + sum(
        math.prod(s.shape) * s.dtype.itemsize for s in shapes
    )
    return pl.pallas_call(
        body,
        out_shape=shapes,
        in_specs=[
            pl.BlockSpec(memory_space=pltpu.HBM if is_hbm(a) else pltpu.VMEM) for a in args
        ],
        out_specs=[pl.BlockSpec(memory_space=pltpu.VMEM)] * len(shapes),
        scratch_shapes=list(scratch),
        compiler_params=pltpu.CompilerParams(vmem_limit_bytes=limit << 20),
        cost_estimate=pl.CostEstimate(flops=0, bytes_accessed=moved, transcendentals=0),
        name=name,
    )(*args)


def taps_matrix(distance, kept):
    a = (math.sqrt(3.0) / 8.0) * jnp.abs(distance).astype(F32)
    value = (tap_scale() * (1.0 + a)) * jnp.exp(-a)
    return jnp.where(kept & (jnp.abs(distance) <= REACH), value, 0.0)


def operators(rows_x, rows_y, depth, hx_ref, hy_ref, hz_ref):
    cells = rows_x * rows_y
    out = iota((cells, cells), 0)
    inp = iota((cells, cells), 1)
    out_x, out_y = out // rows_y, out % rows_y
    inp_x, inp_y = inp // rows_y, inp % rows_y
    near_x = 2 * lax.rem(lax.axis_index("cx"), 2) - 1
    near_y = 2 * lax.rem(lax.axis_index("cy"), 2) - 1
    for at, side in enumerate((0, 1, -1)):
        high, low = split(taps_matrix(out_x - inp_x + side * near_x * rows_x, out_y == inp_y))
        hx_ref[2 * at], hx_ref[2 * at + 1] = high, low
        high, low = split(taps_matrix(out_y - inp_y + side * near_y * rows_y, out_x == inp_x))
        hy_ref[2 * at], hy_ref[2 * at + 1] = high, low
    shift = iota((depth, depth), 0) - iota((depth, depth), 1)
    high, low = split(taps_matrix(shift, shift == shift))
    hz_ref[0], hz_ref[1] = high, low


def one_hot(hits):
    return jnp.where(hits, 1.0, 0.0).astype(BF16)


def fetch(moves, sems):
    copies = [
        pltpu.make_async_copy(src, dst, sems.at[at]) for at, (src, dst) in enumerate(moves)
    ]
    for copy in copies:
        copy.start()
    return copies


def fetch_rays(resp_hbm, first, resp_ref, sems):
    chunk = resp_ref.shape[0] // FETCHES
    return fetch(
        [
            (resp_hbm.at[pl.ds(first + at, chunk)], resp_ref.at[pl.ds(at, chunk)])
            for at in range(0, resp_ref.shape[0], chunk)
        ],
        sems,
    )


def flip_rays(copies, resp_ref, flip_ref):
    tiles, samples, star_tile = resp_ref.shape
    chunk = tiles // FETCHES
    for copy, first in zip(copies, range(0, tiles, chunk)):
        copy.wait()
        rows = resp_ref[first : first + chunk].reshape(chunk * samples, star_tile)
        flip_ref[:, first * samples : (first + chunk) * samples] = rows.T


def operators_body(
    rows_x, rows_y, own_hbm, group_hbm, slot_hbm, resp_hbm,
    hx_ref, hy_ref, hz_ref, part_ref, resp_ref, flip_ref, grp_ref, take_ref, give_ref,
    own_ref, group_ref, slot_ref, keep, sems, ray_sems,
):
    copies = fetch([(own_hbm, own_ref), (group_hbm, group_ref), (slot_hbm, slot_ref)], sems)
    ray_copies = fetch_rays(resp_hbm, 0, resp_ref, ray_sems)
    operators(rows_x, rows_y, hz_ref.shape[1], hx_ref, hy_ref, hz_ref)
    for copy in copies:
        copy.wait()
    part_ref[...] = apply_left(hx_ref[0], hx_ref[1], own_ref[...])
    tiles, slots = take_ref.shape
    keep[...] = jnp.broadcast_to(group_ref[...], (LANES, tiles)).T
    lane_first = iota((tiles // 2, LANES), 1) < LANES // 2
    grp_ref[...] = jnp.where(
        lane_first, keep[pl.ds(0, tiles // 2, 2), :], keep[pl.ds(1, tiles // 2, 2), :]
    )
    slot = slot_ref[...]
    wide = jnp.broadcast_to(slot, (LANES, tiles)).T
    for at in range(0, slots, LANES):
        take_ref[:, at : at + LANES] = one_hot(wide == iota((tiles, LANES), 1) + at)
    give_ref[...] = one_hot(jnp.broadcast_to(slot, (slots, tiles)) == iota((slots, tiles), 0))
    flip_rays(ray_copies, resp_ref, flip_ref)


def tables_body(
    off_hbm, frac_hbm, send_hbm, obs_hbm, sig_hbm, resp_hbm,
    field_ref, hy_ref, hz_ref,
    part_ref, resp_ref, flip_ref, obs_ref, var_ref,
    idx_ref, w_ref, pack_ref, sum_ref,
    off_ref, frac_ref, send_ref, sig_ref, sems, ray_sems,
):
    copies = fetch(
        [
            (off_hbm, off_ref), (frac_hbm, frac_ref), (send_hbm, send_ref),
            (obs_hbm, obs_ref), (sig_hbm, sig_ref),
        ],
        sems,
    )
    first = resp_hbm.shape[0] - resp_ref.shape[0]
    ray_copies = fetch_rays(resp_hbm, first, resp_ref, ray_sems)
    part = apply_left(hy_ref[0], hy_ref[1], field_ref[...])
    part_ref[...] = apply_right(part, hz_ref[0], hz_ref[1])
    for copy in copies:
        copy.wait()
    sig = sig_ref[...]
    var_ref[...] = sig * sig
    slots, cells = pack_ref.shape
    off = off_ref[...]
    frac = frac_ref[...]
    idx_ref[...] = jnp.concatenate([off, off + 1], axis=0).T
    w_ref[...] = jnp.concatenate([1.0 - frac, frac], axis=0).T
    capacity, devices = send_ref.shape
    wide = jnp.concatenate(
        [
            jnp.broadcast_to(send_ref[:, at : at + 1], (capacity, LANES))
            for at in range(devices)
        ],
        axis=0,
    )
    for at in range(0, cells, LANES):
        pack_ref[:, at : at + LANES] = one_hot(wide == iota((slots, LANES), 1) + at)
    send = wide.T[0:1]
    sum_ref[...] = one_hot(jnp.broadcast_to(send, (cells, slots)) == iota((cells, slots), 0))
    flip_rays(ray_copies, resp_ref, flip_ref)


def sides(mats_ref, near, far):
    return apply_left(mats_ref[2], mats_ref[3], near) + apply_left(mats_ref[4], mats_ref[5], far)


def own_body(own_ref, mats_ref, part_ref):
    part_ref[...] = apply_left(mats_ref[0], mats_ref[1], own_ref[...])


def own_latent_body(own_ref, mats_ref, latent_ref, part_ref):
    part_ref[...] = latent_ref[...] + apply_left(mats_ref[0], mats_ref[1], own_ref[...])


def join_body(part_ref, near_ref, far_ref, mats_ref, out_ref, *sent_ref):
    out = part_ref[...] + sides(mats_ref, near_ref[...], far_ref[...])
    out_ref[...] = out
    for ref in sent_ref:
        ref[...] = out.astype(ref.dtype)


def density_body(part_ref, near_ref, far_ref, mats_ref, hz_ref, pack_ref, dens_ref, packed_ref):
    out = sides(mats_ref, near_ref[...], far_ref[...])
    dens = jnp.exp(part_ref[...] + apply_right(out, hz_ref[0], hz_ref[1]))
    dens_ref[...] = dens
    packed_ref[...] = mm(pack_ref[...], dens.astype(BF16)).astype(BF16)


def owner_body(sum_ref, back_ref, dens_ref, hz_ref, out_ref, sent_ref):
    grad = dens_ref[...] * mm(sum_ref[...], back_ref[...])
    out = mm(grad.astype(BF16), hz_ref[0])
    out_ref[...] = out
    sent_ref[...] = out.astype(sent_ref.dtype)


def cone_body(
    got_ref, early_ref, late_ref, flip_early_ref, flip_late_ref, idx_ref, w_ref, grp_ref, take_ref, give_ref, obs_ref, var_ref,
    pred_ref, grad_ref, both, cells,
):
    early, samples, star_tile = early_ref.shape
    tiles = idx_ref.shape[0]
    depth = got_ref.shape[1]
    groups = obs_ref.shape[0]
    half = LANES // 2

    def rays(first, count):
        ref, first = (early_ref, first) if first < early else (late_ref, first - early)
        return ref[first : first + count].reshape(count * samples, star_tile)

    def flipped(first, count):
        ref, first = (flip_early_ref, first) if first < early else (flip_late_ref, first - early)
        return ref[:, first * samples : (first + count) * samples]

    group_at = iota((groups, LANES), 0)
    lane_first = iota((AHEAD // 2, LANES), 1) < half
    got = got_ref[...]
    pred = jnp.zeros((groups, star_tile), F32)
    for base in range(0, tiles, AHEAD):
        span = pl.ds(base, AHEAD)
        idx = idx_ref[span, :]
        columns = mm(take_ref[span, :], got)
        for at in range(0, depth, LANES):
            piece = jnp.take_along_axis(
                columns[:, at : at + LANES], idx & (LANES - 1), axis=1
            )
            value = jnp.where(idx >= at, piece, value) if at else piece
        value = w_ref[span, :] * value
        both[span, :] = value + pltpu.roll(value, half, 1)
    for base in range(0, tiles, AHEAD):
        pair = jnp.where(
            lane_first, both[pl.ds(base, AHEAD // 2, 2), :], both[pl.ds(base + 1, AHEAD // 2, 2), :]
        )
        group = grp_ref[pl.ds(base // 2, AHEAD // 2), :]
        left = [
            jnp.where(group[i : i + 1] == group_at, pair[i : i + 1], 0.0)
            for i in range(AHEAD // 2)
        ]
        pred += mm(jnp.concatenate(left, axis=1).astype(BF16), rays(base, AHEAD))

    pred_ref[...] = pred
    resid = ((pred - obs_ref[...]) / var_ref[...]).astype(BF16)
    parts = depth // PART
    rows = 2 * parts
    at_row = iota((rows, LANES), 0)
    row_part = at_row & (parts - 1)
    row_second = (at_row & parts) != 0
    level = [(iota((16, LANES), 0) + at).astype(F32).astype(BF16) for at in range(0, PART, 16)]
    one = jnp.ones((16, LANES), BF16)
    zero = jnp.zeros((16, LANES), BF16)
    shift = PART.bit_length() - 1
    total = jnp.zeros(grad_ref.shape, F32)
    lane_first = iota((CHUNK // 2, LANES), 1) < half
    for base in range(0, tiles, CHUNK):
        back = mm(resid, flipped(base, CHUNK))
        group = grp_ref[pl.ds(base // 2, CHUNK // 2), :]
        picked = [
            jnp.sum(
                jnp.where(group[i : i + 1] == group_at, back[:, i * LANES : (i + 1) * LANES], 0.0),
                axis=0, keepdims=True,
            )
            for i in range(CHUNK // 2)
        ]
        picked = jnp.concatenate(picked, axis=0)
        swapped = pltpu.roll(picked, half, 1)
        even, odd = pl.ds(base, CHUNK // 2, 2), pl.ds(base + 1, CHUNK // 2, 2)
        weights = (
            jnp.where(lane_first, picked, swapped) * w_ref[even, :],
            jnp.where(lane_first, swapped, picked) * w_ref[odd, :],
        )
        spots = (idx_ref[even, :], idx_ref[odd, :])
        lanes = [(spot & (PART - 1)).astype(F32) for spot in spots]
        blocks = [lax.shift_right_logical(spot, shift) for spot in spots]
        blocks[1] = blocks[1] + parts
        for i in range(CHUNK // 2):
            left, right = [], []
            for which in (0, 1):
                kept = at_row == blocks[which][i : i + 1]
                left.append(jnp.where(kept, weights[which][i : i + 1], 0.0))
                lane = jnp.broadcast_to(lanes[which][i : i + 1], (16, LANES)).astype(BF16)
                right.append(
                    jnp.concatenate([jnp.where(lane == lv, one, zero) for lv in level], axis=0)
                )
            cells[(base // 2 + i) * rows : (base // 2 + i + 1) * rows, :] = mm_nt(
                jnp.concatenate(left, axis=1).astype(BF16), jnp.concatenate(right, axis=1)
            )
        if (base + CHUNK) % GIVE == 0:
            start = base + CHUNK - GIVE
            pieces = [cells[pl.ds(start * parts + at, GIVE, parts), :] for at in range(parts)]
            total += mm(
                give_ref[:, start : start + GIVE], jnp.concatenate(pieces, axis=1).astype(BF16)
            )
    grad_ref[...] = total.astype(BF16)


def cone_scratch(tiles, depth):
    return [pltpu.VMEM((tiles, LANES), F32), pltpu.VMEM((tiles * (depth // PART), PART), F32)]


def exchanged(values, axis):
    count = lax.axis_size(axis)
    return [
        lax.ppermute(
            values, axis,
            [pair for i in range(first, count - 1, 2) for pair in ((i, i + 1), (i + 1, i))],
        )
        for first in (0, 1)
    ]


def on_device(
    latent, observed, sigma, response, offsets, fractions, tile_group, tile_slot, send_index
):
    rows_x, rows_y, depth = latent.shape
    cells = rows_x * rows_y
    axes = ("cx", "cy")
    devices = lax.axis_size("cx") * lax.axis_size("cy")
    slots = devices * send_index.shape[2]
    tiles, samples, star_tile = response.shape
    groups = observed.shape[0] // star_tile
    own = latent.reshape(cells, depth)
    field_out = ((cells, depth), F32)
    sent_out = ((cells, depth), BF16)

    send = send_index.reshape(devices, -1).T
    flip_out = ((star_tile, tiles // 2 * samples), BF16)
    ray_out = ((tiles // 2, samples, star_tile), BF16)
    near, far = exchanged(own.astype(BF16), "cx")
    hx, hy, hz, part, early, flip_early, grp, take, give = call(
        functools.partial(operators_body, rows_x, rows_y),
        [
            ((6, cells, cells), BF16), ((6, cells, cells), BF16), ((2, depth, depth), BF16),
            field_out, ray_out, flip_out,
            ((tiles // 2, LANES), jnp.int32), ((tiles, slots), BF16), ((slots, tiles), BF16),
        ],
        hbm(own), hbm(tile_group.reshape(1, tiles)), hbm(tile_slot.reshape(1, tiles)),
        hbm(response),
        scratch=[
            pltpu.VMEM((cells, depth), F32),
            pltpu.VMEM((1, tiles), jnp.int32),
            pltpu.VMEM((1, tiles), jnp.int32),
            pltpu.VMEM((tiles, LANES), jnp.int32),
            pltpu.SemaphoreType.DMA((3,)),
            pltpu.SemaphoreType.DMA((FETCHES,)),
        ],
        name="operators",
    )
    field, sent = call(join_body, [field_out, sent_out], part, near, far, hx, name="along_x")
    near, far = exchanged(sent, "cy")
    part, late, flip_late, obs, var, idx, weight, pack, add_up = call(
        tables_body,
        [
            field_out,
            ray_out,
            flip_out,
            ((groups, star_tile), F32),
            ((groups, star_tile), F32),
            ((tiles, LANES), jnp.int32),
            ((tiles, LANES), F32),
            ((slots, cells), BF16),
            ((cells, slots), BF16),
        ],
        hbm(offsets), hbm(fractions), hbm(send),
        hbm(observed.reshape(groups, star_tile)), hbm(sigma.reshape(groups, star_tile)),
        hbm(response), field, hy, hz,
        scratch=[
            pltpu.VMEM((samples, tiles), jnp.int32),
            pltpu.VMEM((samples, tiles), F32),
            pltpu.VMEM(send.shape, jnp.int32),
            pltpu.VMEM((groups, star_tile), F32),
            pltpu.SemaphoreType.DMA((5,)),
            pltpu.SemaphoreType.DMA((FETCHES,)),
        ],
        name="tables",
    )
    dens, packed = call(
        density_body, [field_out, ((slots, depth), BF16)],
        part, near, far, hy, hz, pack, name="density",
    )
    got = lax.all_to_all(packed, axes, split_axis=0, concat_axis=0, tiled=True)
    pred, grad = call(
        cone_body, [((groups, star_tile), F32), ((slots, depth), BF16)],
        got, early, late, flip_early, flip_late, idx, weight, grp, take, give, obs, var,
        scratch=cone_scratch(tiles, depth),
        limit=20,
        name="cones",
    )
    back = lax.all_to_all(grad, axes, split_axis=0, concat_axis=0, tiled=True)
    field, sent = call(owner_body, [field_out, sent_out], add_up, back, dens, hz, name="owners")
    near, far = exchanged(sent, "cy")
    (part,) = call(own_body, [field_out], field, hy, name="own_y")
    field, sent = call(join_body, [field_out, sent_out], part, near, far, hy, name="along_y")
    near, far = exchanged(sent, "cx")
    (part,) = call(own_latent_body, [field_out], field, hx, own, name="own_x")
    (gradient,) = call(join_body, [field_out], part, near, far, hx, name="finish")
    return gradient.reshape(rows_x, rows_y, depth), pred.reshape(-1)


def solution(mesh):
    both = ("cx", "cy")
    placed = (
        P("cx", "cy", None),
        P(both),
        P(both),
        P(both, None, None),
        P(None, both),
        P(None, both),
        P(both),
        P(both),
        P(both, None, None),
    )
    return jax.shard_map(
        on_device,
        mesh=mesh,
        in_specs=placed,
        out_specs=(P("cx", "cy", None), P(both)),
        check_vma=False,
    )
```
